512 devices in a mesh: seq: 128 (over z, x, core), head: 4 (over y).
Axes of the slice: x: 4, y: 4, z: 16, core: 2. Of those that a mesh axis runs over, the one named last changes fastest.
Arguments:
- out_grad: bfloat16 [16384, 768], P('seq', 'head'), may hold values from -6 to 6
- expert_of: int32 [16384], P('seq'), may hold values from 0 to 127, as said below
- counts: int32 [128, 128], P(None, 'seq'), may hold values from 0 to 2, as said below
- w_up: bfloat16 [128, 768, 3072], P('seq', None, 'head'), may hold values from -0.21875 to 0.21875
- w_down: bfloat16 [128, 3072, 768], P('seq', 'head'), may hold values from -0.109375 to 0.109375
- pre_act: bfloat16 [32768, 3072], P('seq', 'head'), may hold values from -6 to 6
- queries: bfloat16 [16384, 1024], P('seq', 'head'), may hold values from -6 to 6
- keys: bfloat16 [16384, 1024], P('seq', 'head'), may hold values from -6 to 6
- values: bfloat16 [16384, 1024], P('seq', 'head'), may hold values from -6 to 6
- w_out: bfloat16 [1024, 768], P('head'), may hold values from -0.1875 to 0.1875
Outputs:
- grad_hidden: bfloat16 [16384, 768], P('seq')
- grad_queries: bfloat16 [16384, 1024], P('seq', 'head')
- grad_keys: bfloat16 [16384, 1024], P('seq', 'head')
- grad_values: bfloat16 [16384, 1024], P('seq', 'head')
The draws below stay inside these ranges and needn't reach their ends.
Inputs may be any that keep to these rules, and one draw needn't show every extreme that they name: `expert_of`: in each aligned block of 128 tokens at most 2 tokens name one expert; one expert, the same for every block, is named by exactly 2 tokens of every block, and every other expert by fewer than 2 tokens of a block. counts[s, e] is the number of tokens of block s that name expert e.
All inputs are finite; a program needn't handle non-finite values.
Results may differ from the reference program's by a relative error of at most 0.014.
Values may be sent and summed in bfloat16 or wider, within the bound.
No kernel may reach another device: no remote copies, remote signals or barrier semaphores. Data moves between devices by JAX's collectives and lax.ppermute only.
A program may use at most 64 MiB of HBM per device.

```python
import math
import jax
import jax.numpy as jnp
from jax import lax

D = 768
FF = 3072
HD = 256
TOK_DEV = 128
HEADS = 4
EXPERTS = 128
TOKENS = 16384
CAP = 2
SLOTS = 256
N_HEAD = 4


def route_table(key):
    base_key = jax.random.fold_in(key, 7)
    hot_key, block_key = jax.random.split(base_key)
    hot_expert = jax.random.randint(hot_key, (), 0, EXPERTS)
    block_keys = jax.random.split(block_key, EXPERTS)
    spare_slots = (EXPERTS - 1) * (CAP - 1)

    def one_block(one_key):
        slot_key, order_key = jax.random.split(one_key)
        slot_order = jax.random.permutation(slot_key, spare_slots)
        others = slot_order[:TOK_DEV - CAP] // (CAP - 1)
        others = (others + (others >= hot_expert).astype(jnp.int32)).astype(jnp.int32)
        assigned = jnp.concatenate([jnp.full((CAP,), hot_expert, jnp.int32), others])
        position = jax.random.permutation(order_key, TOK_DEV)
        return assigned[position]
    return jax.vmap(one_block)(block_keys).astype(jnp.int32)


def draw_expert_of(key, part):
    return route_table(key).reshape(-1)


def draw_counts(key, part):
    routes = route_table(key)
    matches = routes[:, :, None] == jnp.arange(EXPERTS, dtype=jnp.int32)[None, None, :]
    return jnp.sum(matches.astype(jnp.int32), axis=1)


def levels(own_key, extent, cuts, smallest, top_value):
    gain = 1.0
    for dim, shards_of in cuts:
        steps = jax.random.uniform(jax.random.fold_in(jax.random.fold_in(own_key, 6), dim), (shards_of,), jnp.float32, smallest / len(cuts), top_value / len(cuts))
        gain = gain * jnp.repeat(jnp.exp(steps), extent[dim] // shards_of).reshape((-1,) + (1,) * (len(extent) - 1 - dim))
    return gain


def gaussian(key, dims, scale, bound, cuts=(), held_as=jnp.bfloat16):
    array = scale * jax.random.normal(key, dims, jnp.float32)
    if cuts:
        array = array * levels(key, dims, cuts, -0.22, 0.18)
    return jnp.clip(array, -bound, bound).astype(held_as)


def setup_inputs(seed: int = 0) -> dict:
    seeds = jax.random.split(jax.random.key(seed), 11)
    return {
        "out_grad": gaussian(seeds[0], (TOKENS, D), 1.0, 6.0, ((0, 128), (1, 4))),
        "expert_of": draw_expert_of(jax.random.fold_in(seeds[10], 71), 0),
        "counts": draw_counts(jax.random.fold_in(seeds[10], 71), 0),
        "w_up": gaussian(seeds[3], (EXPERTS, D, FF), D ** -0.5, 0.21875, ((0, 128), (2, 4))),
        "w_down": gaussian(seeds[4], (EXPERTS, FF, D), FF ** -0.5, 0.109375, ((0, 128), (1, 4))),
        "pre_act": gaussian(seeds[5], (EXPERTS * SLOTS, FF), 1.0, 6.0, ((0, 128), (1, 4))),
        "queries": gaussian(seeds[6], (TOKENS, HEADS * HD), 1.0, 6.0, ((0, 128), (1, 4))),
        "keys": gaussian(seeds[7], (TOKENS, HEADS * HD), 1.0, 6.0, ((0, 128), (1, 4))),
        "values": gaussian(seeds[8], (TOKENS, HEADS * HD), 1.0, 6.0, ((0, 128), (1, 4))),
        "w_out": gaussian(seeds[9], (HEADS * HD, D), (HEADS * HD) ** -0.5, 0.1875, ((0, 4),)),
    }


def reference(out_grad, expert_of, counts, w_up, w_down, pre_act, queries, keys, values, w_out):
    blocks = expert_of.reshape(EXPERTS, TOK_DEV)
    onehot = (blocks[:, :, None] == jnp.arange(EXPERTS, dtype=jnp.int32)[None, None, :]).astype(jnp.int32)
    token_rank = lax.optimization_barrier(jnp.sum((jnp.cumsum(onehot, axis=1) - 1) * onehot, axis=2))
    offsets = jnp.cumsum(counts, axis=0) - counts
    base_row = jnp.take_along_axis(offsets, blocks, axis=1)
    packed = (blocks * SLOTS + base_row + token_rank).reshape(-1).astype(jnp.int32)
    row_table = jnp.full((EXPERTS * SLOTS,), TOKENS, jnp.int32).at[packed].set(jnp.arange(TOKENS, dtype=jnp.int32))
    padded = jnp.concatenate([out_grad, jnp.zeros((1, D), out_grad.dtype)], axis=0)
    rows_in = padded[row_table].reshape(EXPERTS, SLOTS, D)
    pre_blocks = pre_act.reshape(EXPERTS, SLOTS, FF)
    quarter = FF // N_HEAD

    def expert_step(inputs):
        row_block, pre_block, up_weight, down_weight = inputs
        middle = jnp.dot(row_block, down_weight.T, preferred_element_type=jnp.float32)
        mid_grad = jnp.where(pre_block > 0, middle, jnp.zeros_like(middle)).astype(jnp.bfloat16)
        summed = jnp.zeros((SLOTS, D), jnp.float32)
        for part_index in range(N_HEAD):
            lower = part_index * quarter
            term = jnp.dot(mid_grad[:, lower:lower + quarter], up_weight[:, lower:lower + quarter].T, preferred_element_type=jnp.float32).astype(jnp.bfloat16)
            term = lax.optimization_barrier(term)
            summed = summed + term.astype(jnp.float32)
        return summed.astype(jnp.bfloat16)
    expert_packed = lax.map(expert_step, (rows_in, pre_blocks, w_up, w_down))
    expert_grad = expert_packed.reshape(EXPERTS * SLOTS, D)[packed]
    grad_hidden = (out_grad.astype(jnp.float32) + expert_grad.astype(jnp.float32)).astype(jnp.bfloat16)
    head_grad = jnp.dot(grad_hidden, w_out.T, preferred_element_type=jnp.float32).astype(jnp.bfloat16)
    query_heads = queries.astype(jnp.float32).reshape(TOKENS, HEADS, HD)
    key_heads = keys.astype(jnp.float32).reshape(TOKENS, HEADS, HD)
    value_heads = values.astype(jnp.float32).reshape(TOKENS, HEADS, HD)
    grad_heads = head_grad.astype(jnp.float32).reshape(TOKENS, HEADS, HD)
    key_state = jnp.einsum('tha,thb->hab', key_heads, value_heads)
    query_state = jnp.einsum('tha,thb->hab', query_heads, grad_heads)
    key_round = lax.optimization_barrier(key_state.astype(jnp.bfloat16)).astype(jnp.float32)
    query_round = lax.optimization_barrier(query_state.astype(jnp.bfloat16)).astype(jnp.float32)
    scaling = 1.0 / math.sqrt(HD * TOKENS)
    grad_queries = (scaling * jnp.einsum('thb,hab->tha', grad_heads, key_round)).reshape(TOKENS, HEADS * HD)
    grad_keys = (scaling * jnp.einsum('thb,hab->tha', value_heads, query_round)).reshape(TOKENS, HEADS * HD)
    grad_values = (scaling * jnp.einsum('tha,hab->thb', key_heads, query_round)).reshape(TOKENS, HEADS * HD)
    return (grad_hidden, grad_queries.astype(jnp.bfloat16), grad_keys.astype(jnp.bfloat16), grad_values.astype(jnp.bfloat16))
```

```python
import math

import jax
import jax.numpy as jnp
from jax import lax
from jax.experimental import pallas as pl
from jax.experimental.pallas import tpu as pltpu
from jax.sharding import Mesh
from jax.sharding import PartitionSpec as P

SEQ = ("z", "x", "c")
PLANE = ("x", "c")
BF, F32 = jnp.bfloat16, jnp.float32
NZ, NP, NH = 16, 8, 4
BLOCK = 128
D, HD, DQ = 768, 256, 192
VMEM = pl.BlockSpec(memory_space=pltpu.VMEM)


def nn(a, b):
    return lax.dot_general(a, b, (((1,), (0,)), ((), ())), preferred_element_type=F32)


def nt(a, b):
    return lax.dot_general(a, b, (((1,), (1,)), ((), ())), preferred_element_type=F32)


def tn(a, b):
    return lax.dot_general(a, b, (((0,), (0,)), ((), ())), preferred_element_type=F32)


def hot(cond):
    return jnp.where(cond, 1.0, 0.0).astype(BF)


def iota(shape, dim):
    return lax.broadcasted_iota(jnp.int32, shape, dim)


def halves(state):
    parts = state.reshape(NP, 2, 16, HD)
    return parts[:, 0], parts[:, 1]


def call(kernel, outs, *args, flops=10**8):
    single = not isinstance(outs, (list, tuple))
    shapes = [outs] if single else list(outs)
    nbytes = sum(a.size * a.dtype.itemsize for a in args)
    res = pl.pallas_call(
        kernel,
        out_shape=shapes,
        in_specs=[VMEM] * len(args),
        out_specs=[VMEM] * len(shapes),
        cost_estimate=pl.CostEstimate(flops=flops, bytes_accessed=nbytes, transcendentals=0),
        name=kernel.__name__,
    )(*args)
    return res[0] if single else res


def sds(*shape, dtype=BF):
    return jax.ShapeDtypeStruct(shape, dtype)


def pack(e_ref, og_ref, q_ref, out_ref):
    e = e_ref[...]
    pos = (e & 7) * NZ + (e >> 3)
    match = pos == iota((BLOCK, BLOCK), 0)
    upper = hot(iota((BLOCK, BLOCK), 0) < iota((BLOCK, BLOCK), 1))
    prev = nn(hot(match), upper)
    first = hot(match & (prev < 0.5))
    second = hot(match & (prev >= 0.5))
    og, q = og_ref[...], q_ref[...]
    out_ref[:, 0:384] = jnp.concatenate([nn(first, og), nn(second, og)], axis=1).astype(BF)
    out_ref[:, 384:640] = nn(first, q).astype(BF)
    out_ref[:, 640:896] = nn(second, q).astype(BF)


def prepare(c_ref, pre_ref, k_ref, v_ref, mask_ref, kst_ref):
    c = c_ref[...].astype(F32)
    p = iota((BLOCK, BLOCK), 0)
    s_of_p = (p & (NZ - 1)) * NP + (p >> 4)
    s = iota((BLOCK, BLOCK), 1)
    zero = jnp.zeros((BLOCK, BLOCK), F32)
    offset = jnp.sum(jnp.where(s < s_of_p, c, zero), axis=1, keepdims=True)
    count = jnp.sum(jnp.where(s == s_of_p, c, zero), axis=1, keepdims=True)
    row = iota((BLOCK, 2 * BLOCK), 1).astype(F32)
    live = jnp.where(pre_ref[...].astype(F32) > 0, 1.0, 0.0).astype(BF)
    for r in range(2):
        pick = hot((row == offset + r) & (count > r + 0.5))
        mask_ref[r] = nn(pick, live).astype(BF)
    a, b = halves(tn(k_ref[...], v_ref[...]))
    kst_ref[:, :, 0:HD] = a.astype(BF)
    kst_ref[:, :, HD:] = b.astype(BF)


def experts(rows_ref, mask_ref, wd_ref, wu_ref, full_ref, parts_ref):
    wd, wu = wd_ref[...], wu_ref[...]
    for r in range(2):
        x = jnp.concatenate([rows_ref[h, :, r * DQ : (r + 1) * DQ] for h in range(NH)], axis=1)
        full_ref[r] = x
        mid = jnp.where(mask_ref[r].astype(F32) > 0.5, nt(x, wd), 0.0).astype(BF)
        part = nt(mid, wu).astype(BF)
        for h in range(NH):
            parts_ref[h, r] = part


def combine(parts_ref, full_ref, recv_ref, wo_ref, kst_ref, out_ref):
    wo = wo_ref[...]
    state = jnp.zeros((HD, HD), F32)
    for r in range(2):
        total = parts_ref[0, r].astype(F32)
        for h in range(1, NH):
            total = total + parts_ref[h, r].astype(F32)
        gh = (full_ref[r].astype(F32) + total.astype(BF).astype(F32)).astype(BF)
        hg = nt(gh, wo).astype(BF)
        state = state + tn(recv_ref[:, 384 + r * HD : 384 + (r + 1) * HD], hg)
        out_ref[:, :, r * D : (r + 1) * D] = gh.reshape(NP, 16, D)
    a, b = halves(state)
    out_ref[:, :, 1536:1792] = a.astype(BF)
    out_ref[:, :, 1792:2048] = b.astype(BF)
    out_ref[:, :, 2048:2560] = kst_ref[...]


def regroup(in_ref, out_ref):
    total = in_ref[0, :, 1536:2560].astype(F32)
    for i in range(1, NP):
        total = total + in_ref[i, :, 1536:2560].astype(F32)
    out_ref[:, :, 0:1024] = jnp.broadcast_to(total.astype(BF)[None], (NZ, 16, 1024))
    x0 = in_ref[:, :, 0:D].reshape(BLOCK, D)
    x1 = in_ref[:, :, D : 2 * D].reshape(BLOCK, D)
    o = iota((2 * BLOCK, BLOCK), 0)
    i = iota((2 * BLOCK, BLOCK), 1)
    same = ((o & 7) == (i >> 4)) & ((o >> 4) == (i & 15))
    lower = hot(same & ((o & 8) == 0))
    higher = hot(same & ((o & 8) != 0))
    rows = nn(lower, x0[:, 0:384]) + nn(higher, x0[:, 384:768])
    out_ref[:, :, 1024:1408] = rows.astype(BF).reshape(NZ, 16, 384)
    seconds = jnp.zeros((2 * BLOCK, 128), F32)
    for j in range(6):
        pick = hot(((o & 15) == j) & ((o >> 4) == (i & 15)))
        seconds = seconds + nn(pick, x1[:, j * 128 : (j + 1) * 128])
    out_ref[:, :, 1408:1536] = seconds.astype(BF).reshape(NZ, 16, 128)


def reduce_states(in_ref, out_ref):
    total = in_ref[0, :, 0:1024].astype(F32)
    for i in range(1, NZ):
        total = total + in_ref[i, :, 0:1024].astype(F32)
    out_ref[...] = jnp.broadcast_to(total.astype(BF)[None], (NP, 16, 1024))


def unpack(in_ref, erow_ref, ecol_ref, wo_ref, gh_ref, hg_ref):
    e = ecol_ref[...]
    earlier = iota((BLOCK, BLOCK), 1) < iota((BLOCK, BLOCK), 0)
    twice = jnp.where((e == erow_ref[...]) & earlier, 1.0, 0.0)
    rank = jnp.sum(twice, axis=1, keepdims=True)
    lane = iota((BLOCK, 2 * BLOCK), 1)
    same = (e == (lane >> 4) * NP + (lane & 7)) & (rank < 0.5)
    lower = hot(same & ((lane & 8) == 0))
    higher = hot(same & ((lane & 8) != 0))
    rows = in_ref[:, :, 1024:1408].reshape(2 * BLOCK, 384)
    seconds = in_ref[0, :, 1408:1536].astype(F32)
    for i in range(1, NZ):
        seconds = seconds + in_ref[i, :, 1408:1536].astype(F32)
    second = jnp.concatenate([seconds[j : j + 1] for j in range(6)], axis=1)
    gh = jnp.concatenate([nn(lower, rows), nn(higher, rows)], axis=1)
    gh = (gh + jnp.where(rank > 0.5, second, 0.0)).astype(BF)
    gh_ref[...] = gh
    hg_ref[...] = nt(gh, wo_ref[...]).astype(BF)


def finish(in_ref, hg_ref, k_ref, v_ref, gq_ref, gk_ref, gv_ref):
    scaling = 1.0 / math.sqrt(HD * BLOCK * BLOCK)

    def whole(at):
        a = in_ref[:, :, at : at + HD].reshape(NP, 1, 16, HD)
        b = in_ref[:, :, at + HD : at + 2 * HD].reshape(NP, 1, 16, HD)
        return jnp.concatenate([a, b], axis=1).reshape(HD, HD)

    qr, kr = whole(0), whole(512)
    gq_ref[...] = (scaling * nt(hg_ref[...], kr)).astype(BF)
    gk_ref[...] = (scaling * nt(v_ref[...], qr)).astype(BF)
    gv_ref[...] = (scaling * nn(k_ref[...], qr)).astype(BF)


def swap(tiles, axis):
    return lax.all_to_all(tiles, axis, split_axis=0, concat_axis=0, tiled=True)


def shards(out_grad, expert_of, counts, w_up, w_down, pre_act, queries, keys, values, w_out):
    e_row = expert_of.reshape(1, BLOCK)
    e_col = expert_of.reshape(BLOCK, 1)
    send = call(pack, sds(BLOCK, 896), e_row, out_grad, queries)
    recv = swap(send, ("x", "c", "z"))
    mask, kst = call(
        prepare,
        [sds(2, BLOCK, D), sds(NP, 16, 2 * HD)],
        counts.reshape(1, BLOCK),
        pre_act,
        keys,
        values,
    )
    rows = swap(jnp.broadcast_to(recv[None, :, 0:384], (NH, BLOCK, 384)), "y")
    full, parts = call(
        experts,
        [sds(2, BLOCK, D), sds(NH, 2, BLOCK, D)],
        rows,
        mask,
        w_down[0],
        w_up[0],
    )
    parts = swap(parts.reshape(NH, 2 * BLOCK, D), "y").reshape(NH, 2, BLOCK, D)
    back = call(combine, sds(NP, 16, 2560), parts, full, recv, w_out, kst)
    back = swap(back, PLANE)
    back = call(regroup, sds(NZ, 16, 1536), back)
    back = swap(back, "z")
    states = call(reduce_states, sds(NP, 16, 1024), back)
    states = swap(states, PLANE)
    gh, hg = call(unpack, [sds(BLOCK, D), sds(BLOCK, HD)], back, e_row, e_col, w_out)
    gq, gk, gv = call(finish, [sds(BLOCK, HD)] * 3, states, hg, keys, values)
    return gh, gq, gk, gv


def solution(mesh):
    finer = Mesh(mesh.devices.reshape(16, 4, 2, mesh.shape["head"]), ("z", "x", "c", "y"))
    return jax.shard_map(
        shards,
        mesh=finer,
        in_specs=(
            P(SEQ, "y"),
            P(SEQ),
            P(None, SEQ),
            P(SEQ, None, "y"),
            P(SEQ, "y", None),
            P(SEQ, "y"),
            P(SEQ, "y"),
            P(SEQ, "y"),
            P(SEQ, "y"),
            P("y", None),
        ),
        out_specs=(P(SEQ, None), P(SEQ, "y"), P(SEQ, "y"), P(SEQ, "y")),
        check_vma=False,
    )
```

```python
import math

import jax
import jax.numpy as jnp
from jax import lax
from jax.experimental import pallas as pl
from jax.experimental.pallas import tpu as pltpu
from jax.sharding import Mesh
from jax.sharding import PartitionSpec as P

SEQ = ("z", "x", "c")
PLANE = ("x", "c")
BF, F32 = jnp.bfloat16, jnp.float32
NZ, NP, NH = 16, 8, 4
BLOCK = 128
D, HD, DQ = 768, 256, 192
LIMIT = 16 * 2**20
VMEM = pl.BlockSpec(memory_space=pltpu.VMEM)


def nn(a, b):
    return lax.dot_general(a, b, (((1,), (0,)), ((), ())), preferred_element_type=F32)


def nt(a, b):
    return lax.dot_general(a, b, (((1,), (1,)), ((), ())), preferred_element_type=F32)


def tn(a, b):
    return lax.dot_general(a, b, (((0,), (0,)), ((), ())), preferred_element_type=F32)


def hot(cond):
    return jnp.where(cond, 1.0, 0.0).astype(BF)


def iota(shape, dim):
    return lax.broadcasted_iota(jnp.int32, shape, dim)


def halves(state):
    parts = state.reshape(NP, 2, 16, HD)
    return parts[:, 0], parts[:, 1]


def call(kernel, outs, *args, far=(), home=False):
    single = not isinstance(outs, (list, tuple))
    shapes = [outs] if single else list(outs)
    nbytes = sum(a.size * a.dtype.itemsize for a in args)
    near = pltpu.with_memory_space_constraint
    res = pl.pallas_call(
        kernel,
        out_shape=shapes if home else [pltpu.VMEM(s.shape, s.dtype) for s in shapes],
        in_specs=[VMEM] * len(args),
        out_specs=[VMEM] * len(shapes),
        cost_estimate=pl.CostEstimate(flops=10**8, bytes_accessed=nbytes, transcendentals=0),
        compiler_params=pltpu.CompilerParams(vmem_limit_bytes=LIMIT),
        name=kernel.__name__,
    )(*[near(a, pltpu.HBM if n in far else pltpu.VMEM) for n, a in enumerate(args)])
    return res[0] if single else res


def sds(*shape, dtype=BF):
    return jax.ShapeDtypeStruct(shape, dtype)


def eye(n):
    return hot(iota((n, n), 0) == iota((n, n), 1))


def repeats(e):
    match = (e & 7) * NZ + (e >> 3) == iota((BLOCK, BLOCK), 0)
    earlier = hot(iota((BLOCK, BLOCK), 0) < iota((BLOCK, BLOCK), 1))
    return match, jnp.where(match & (nn(hot(match), earlier) > 0.5), 1.0, 0.0)


def pack(e_ref, ogt_ref, q_ref, k_ref, v_ref, out_ref):
    match, again = repeats(e_ref[...])
    first = (jnp.where(match, 1.0, 0.0) - again).astype(BF)
    second = jnp.broadcast_to(jnp.sum(again, axis=0, keepdims=True), (16, BLOCK)).astype(BF)
    ogt, q = ogt_ref[...], q_ref[...]
    token = jnp.concatenate([nt(second, ogt), nn(second, q)], axis=1)
    spare = jnp.concatenate(
        [token[0:1, i * 64 : (i + 1) * 64] for i in range(7)] + [jnp.zeros((9, 64), F32)], axis=0
    )
    spare = jnp.broadcast_to(spare[None], (NP, 16, 64)).reshape(BLOCK, 64)
    rows = jnp.concatenate([nt(first, ogt), nn(first, q), spare], axis=1)
    out_ref[:, :, 0:512] = rows.astype(BF).reshape(NP, 16, 512)
    a, b = halves(tn(k_ref[...], v_ref[...]))
    out_ref[:, :, 512:768] = a.astype(BF)
    out_ref[:, :, 768:1024] = b.astype(BF)


def tile_of(z):
    a, b = z // 4, z % 4
    return (a % 2) * 8, (a // 2) * HD + b * 64


def forward(in_ref, out_ref):
    x = in_ref[:, :, 0:512].reshape(BLOCK, 512)
    o = iota((2 * BLOCK, BLOCK), 0)
    i = iota((2 * BLOCK, BLOCK), 1)
    own = ((o & 7) == (i >> 4)) & ((o & 8) == 0) & ((o >> 4) == (i & 15))
    firsts = nn(hot(own), x[:, 0:448])
    other = ((o & 7) == (i >> 4)) & ((o & 8) != 0)
    spare = x[:, 448:512]
    seconds = jnp.concatenate([nn(hot(other & ((i & 15) == j)), spare) for j in range(7)], axis=1)
    total = in_ref[0, :, 512:1024].astype(F32)
    for p in range(1, NP):
        total = total + in_ref[p, :, 512:1024].astype(F32)
    nothing = jnp.zeros((8, 64), F32)
    pieces = []
    for z in range(NZ):
        row, lane = tile_of(z)
        pieces += [total[row : row + 8, lane : lane + 64], nothing]
    rows = jnp.concatenate([firsts + seconds, jnp.concatenate(pieces, axis=0)], axis=1)
    out_ref[...] = rows.astype(BF).reshape(NZ, 16, 512)


def place(c):
    shape = (2 * BLOCK, BLOCK)
    o, s = iota(shape, 0), iota(shape, 1)
    block = (o >> 4) * NP + (o & 7)
    c = jnp.broadcast_to(c, shape)
    before = jnp.sum(jnp.where(s < block, c, 0.0), axis=1, keepdims=True)
    count = jnp.sum(jnp.where(s == block, c, 0.0), axis=1, keepdims=True)
    r = ((iota((2 * BLOCK, 1), 0) >> 3) & 1).astype(F32)
    return before + r, count > r + 0.5


def masks(c_ref, pre_ref, mask_ref):
    row, live = place(c_ref[...].astype(F32))
    pick = hot((iota((2 * BLOCK, 2 * BLOCK), 1).astype(F32) == row) & live)
    on = jnp.where(pre_ref[...].astype(F32) > 0, 1.0, 0.0).astype(BF)
    mask_ref[...] = jnp.transpose(nn(pick, on)).astype(BF)


def arrive(in_ref, c_ref, out_ref, key_ref):
    _, live = place(c_ref[...].astype(F32))
    x = in_ref[:, :, 0:DQ].reshape(2 * BLOCK, DQ).astype(F32)
    x = jnp.where(live, x, 0.0).astype(BF)
    x = nt(eye(DQ), x).astype(BF)
    out_ref[...] = jnp.broadcast_to(x[None], (NH, DQ, 2 * BLOCK))
    total = in_ref[0, 0:8, 448:512].astype(F32)
    for z in range(1, NZ):
        total = total + in_ref[z, 0:8, 448:512].astype(F32)
    key_ref[...] = total.astype(BF)


def experts(rows_ref, mask_ref, wd_ref, wu_ref, out_ref):
    x = rows_ref[...].reshape(D, 2 * BLOCK)
    mid = jnp.where(mask_ref[...].astype(F32) > 0.5, nn(wd_ref[...], x), 0.0).astype(BF)
    out_ref[...] = nn(wu_ref[...], mid).astype(BF).reshape(NH, DQ, 2 * BLOCK)


def add_up(parts_ref, rows_ref, out_ref):
    total = parts_ref[0].astype(F32)
    for h in range(1, NH):
        total = total + parts_ref[h].astype(F32)
    gh = (rows_ref[0].astype(F32) + total.astype(BF).astype(F32)).astype(BF)
    out_ref[...] = jnp.broadcast_to(gh[None], (NH, DQ, 2 * BLOCK))


def combine(all_ref, own_ref, recv_ref, wo_ref, out_ref):
    gh = all_ref[...].reshape(D, 2 * BLOCK)
    hg = nn(wo_ref[...], gh).astype(BF)
    q = recv_ref[:, :, DQ:448].reshape(2 * BLOCK, HD)
    a, b = halves(nn(hg, q))
    o = iota((BLOCK, 2 * BLOCK), 0)
    i = iota((BLOCK, 2 * BLOCK), 1)
    same = ((o >> 4) == (i & 7)) & ((o & 15) == (i >> 4))
    own = own_ref[0]
    firsts = nt(hot(same & ((i & 8) == 0)), own)
    seconds = nt(hot(same & ((i & 8) != 0)), own)
    rows = jnp.concatenate([firsts, seconds], axis=1)
    out_ref[:, :, 0:384] = rows.astype(BF).reshape(NP, 16, 384)
    out_ref[:, :, 384:640] = a.astype(BF)
    out_ref[:, :, 640:896] = b.astype(BF)


def regroup(in_ref, key_ref, out_ref):
    total = in_ref[0, :, 384:896].astype(F32)
    for p in range(1, NP):
        total = total + in_ref[p, :, 384:896].astype(F32)
    out_ref[:, :, 0:512] = jnp.broadcast_to(total.astype(BF)[None], (NZ, 16, 512))
    o = iota((2 * BLOCK, BLOCK), 0)
    i = iota((2 * BLOCK, BLOCK), 1)
    here = (o >> 4) == (i & 15)
    firsts = nn(hot(here & ((o & 15) == (i >> 4))), in_ref[:, :, 0:DQ].reshape(BLOCK, DQ))
    second = nn(hot(here & ((o & 15) == 8)), in_ref[:, :, DQ : 2 * DQ].reshape(BLOCK, DQ))
    key = jnp.concatenate([key_ref[...].astype(F32), jnp.zeros((8, 64), F32)], axis=0)
    key = jnp.broadcast_to(key[None], (NZ, 16, 64)).reshape(2 * BLOCK, 64)
    rows = jnp.concatenate([firsts + second, key], axis=1)
    out_ref[:, :, 512:768] = rows.astype(BF).reshape(NZ, 16, 256)


def reduce_states(in_ref, out_ref):
    total = in_ref[0, :, 0:512].astype(F32)
    for z in range(1, NZ):
        total = total + in_ref[z, :, 0:512].astype(F32)
    upper = [None] * 8
    lower = [None] * 8
    for z in range(NZ):
        row, lane = tile_of(z)
        (lower if row else upper)[lane // 64] = in_ref[z, 0:8, 704:768].astype(F32)
    key = jnp.concatenate(
        [jnp.concatenate(upper, axis=1), jnp.concatenate(lower, axis=1)], axis=0
    )
    out_ref[:, :, 0:512] = jnp.broadcast_to(total.astype(BF)[None], (NP, 16, 512))
    out_ref[:, :, 512:1024] = jnp.broadcast_to(key.astype(BF)[None], (NP, 16, 512))


def unpack(in_ref, e_ref, out_ref):
    e = e_ref[...]
    match, again = repeats(e)
    rank = jnp.sum(again, axis=0, keepdims=True)
    row = iota((2 * BLOCK, BLOCK), 0)
    slot = row & 15
    first = (slot == (e & 7)) & ((row >> 4) == (e >> 3)) & (rank < 0.5)
    second = (slot == 8) & (rank > 0.5)
    rows = in_ref[:, :, 512 : 512 + DQ].reshape(2 * BLOCK, DQ)
    gh = tn(rows, hot(first | second)).astype(BF)
    out_ref[...] = jnp.broadcast_to(gh[None], (NH, DQ, BLOCK))


def finish(in_ref, all_ref, wo_ref, k_ref, v_ref, gh_ref, gq_ref, gk_ref, gv_ref):
    scaling = 1.0 / math.sqrt(HD * BLOCK * BLOCK)

    def whole(at):
        a = in_ref[:, :, at : at + HD].reshape(NP, 1, 16, HD)
        b = in_ref[:, :, at + HD : at + 2 * HD].reshape(NP, 1, 16, HD)
        return jnp.concatenate([a, b], axis=1).reshape(HD, HD)

    qt, kr = whole(0), whole(512)
    gh = nt(eye(BLOCK), all_ref[...].reshape(D, BLOCK)).astype(BF)
    gh_ref[...] = gh
    hg = nt(gh, wo_ref[...]).astype(BF)
    gq_ref[...] = (scaling * nt(hg, kr)).astype(BF)
    gk_ref[...] = (scaling * nn(v_ref[...], qt)).astype(BF)
    gv_ref[...] = (scaling * nt(k_ref[...], qt)).astype(BF)


def swap(tiles, axis):
    return lax.all_to_all(tiles, axis, split_axis=0, concat_axis=0, tiled=True)


def shards(out_grad, expert_of, counts, w_up, w_down, pre_act, queries, keys, values, w_out):
    e = expert_of.reshape(1, BLOCK)
    c = counts.reshape(1, BLOCK)
    rows_t = sds(NH, DQ, 2 * BLOCK)
    sent = call(pack, sds(NP, 16, 1024), e, out_grad.T, queries, keys, values, far=range(5))
    sent = call(forward, sds(NZ, 16, 512), swap(sent, PLANE))
    recv = swap(sent, "z")
    mask = call(masks, sds(D, 2 * BLOCK), c, pre_act, far=(0, 1))
    own, key = call(arrive, [rows_t, sds(8, 64)], recv, c, far=(1,))
    parts = call(experts, rows_t, swap(own, "y"), mask, w_down[0], w_up[0])
    own = call(add_up, rows_t, swap(parts, "y"), own)
    back = call(combine, sds(NP, 16, 896), swap(own, "y"), own, recv, w_out)
    back = call(regroup, sds(NZ, 16, 768), swap(back, PLANE), key)
    back = swap(back, "z")
    states = call(reduce_states, sds(NP, 16, 1024), back)
    own = call(unpack, sds(NH, DQ, BLOCK), back, e, far=(1,))
    states, rows = swap(states, PLANE), swap(own, "y")
    outs = [sds(BLOCK, D)] + [sds(BLOCK, HD)] * 3
    return tuple(call(finish, outs, states, rows, w_out, keys, values, home=True))


def solution(mesh):
    finer = Mesh(mesh.devices.reshape(16, 4, 2, mesh.shape["head"]), ("z", "x", "c", "y"))
    return jax.shard_map(
        shards,
        mesh=finer,
        in_specs=(
            P(SEQ, "y"),
            P(SEQ),
            P(None, SEQ),
            P(SEQ, None, "y"),
            P(SEQ, "y", None),
            P(SEQ, "y"),
            P(SEQ, "y"),
            P(SEQ, "y"),
            P(SEQ, "y"),
            P("y", None),
        ),
        out_specs=(P(SEQ, None), P(SEQ, "y"), P(SEQ, "y"), P(SEQ, "y")),
        check_vma=False,
    )
```

```python
import math

import jax
import jax.numpy as jnp
from jax import lax
from jax.experimental import pallas as pl
from jax.experimental.pallas import tpu as pltpu
from jax.sharding import Mesh
from jax.sharding import PartitionSpec as P

SEQ = ("z", "x", "c")
PLANE = ("x", "c")
BF, F32 = jnp.bfloat16, jnp.float32
NZ, NP, NH = 16, 8, 4
BLOCK = 128
D, HD, DQ = 768, 256, 192
LIMIT = 16 * 2**20
VMEM = pl.BlockSpec(memory_space=pltpu.VMEM)


def nn(a, b):
    return lax.dot_general(a, b, (((1,), (0,)), ((), ())), preferred_element_type=F32)


def nt(a, b):
    return lax.dot_general(a, b, (((1,), (1,)), ((), ())), preferred_element_type=F32)


def tn(a, b):
    return lax.dot_general(a, b, (((0,), (0,)), ((), ())), preferred_element_type=F32)


def hot(cond):
    return jnp.where(cond, 1.0, 0.0).astype(BF)


def iota(shape, dim):
    return lax.broadcasted_iota(jnp.int32, shape, dim)


def halves(state):
    parts = state.reshape(NP, 2, 16, HD)
    return parts[:, 0], parts[:, 1]


def call(kernel, outs, *args, far=(), home=0):
    single = not isinstance(outs, (list, tuple))
    shapes = [outs] if single else list(outs)
    nbytes = sum(a.size * a.dtype.itemsize for a in args)
    near = pltpu.with_memory_space_constraint
    res = pl.pallas_call(
        kernel,
        out_shape=[s if n < home else pltpu.VMEM(s.shape, s.dtype) for n, s in enumerate(shapes)],
        in_specs=[VMEM] * len(args),
        out_specs=[VMEM] * len(shapes),
        cost_estimate=pl.CostEstimate(flops=10**8, bytes_accessed=nbytes, transcendentals=0),
        compiler_params=pltpu.CompilerParams(vmem_limit_bytes=LIMIT),
        name=kernel.__name__,
    )(*[near(a, pltpu.HBM if n in far else pltpu.VMEM) for n, a in enumerate(args)])
    return res[0] if single else res


def sds(*shape, dtype=BF):
    return jax.ShapeDtypeStruct(shape, dtype)


def eye(n):
    return hot(iota((n, n), 0) == iota((n, n), 1))


def repeats(e):
    match = (e & 7) * NZ + (e >> 3) == iota((BLOCK, BLOCK), 0)
    earlier = hot(iota((BLOCK, BLOCK), 0) < iota((BLOCK, BLOCK), 1))
    return match, jnp.where(match & (nn(hot(match), earlier) > 0.5), 1.0, 0.0)


def pack(e_ref, ogt_ref, q_ref, k_ref, v_ref, out_ref):
    match, again = repeats(e_ref[...])
    first = (jnp.where(match, 1.0, 0.0) - again).astype(BF)
    second = jnp.broadcast_to(jnp.sum(again, axis=0, keepdims=True), (16, BLOCK)).astype(BF)
    ogt, q = ogt_ref[...], q_ref[...]
    token = jnp.concatenate([nt(second, ogt), nn(second, q)], axis=1)
    spare = jnp.concatenate(
        [token[0:1, i * 64 : (i + 1) * 64] for i in range(7)] + [jnp.zeros((9, 64), F32)], axis=0
    )
    spare = jnp.broadcast_to(spare[None], (NP, 16, 64)).reshape(BLOCK, 64)
    rows = jnp.concatenate([nt(first, ogt), nn(first, q), spare], axis=1)
    out_ref[:, :, 0:512] = rows.astype(BF).reshape(NP, 16, 512)
    a, b = halves(tn(k_ref[...], v_ref[...]))
    out_ref[:, :, 512:768] = a.astype(BF)
    out_ref[:, :, 768:1024] = b.astype(BF)


def tile_of(z):
    a, b = z // 4, z % 4
    return (a % 2) * 8, (a // 2) * HD + b * 64


def forward(in_ref, out_ref):
    x = in_ref[:, :, 0:512].reshape(BLOCK, 512)
    o = iota((2 * BLOCK, BLOCK), 0)
    i = iota((2 * BLOCK, BLOCK), 1)
    own = ((o & 7) == (i >> 4)) & ((o & 8) == 0) & ((o >> 4) == (i & 15))
    firsts = nn(hot(own), x[:, 0:448])
    other = ((o & 7) == (i >> 4)) & ((o & 8) != 0)
    spare = x[:, 448:512]
    seconds = jnp.concatenate([nn(hot(other & ((i & 15) == j)), spare) for j in range(7)], axis=1)
    total = in_ref[0, :, 512:1024].astype(F32)
    for p in range(1, NP):
        total = total + in_ref[p, :, 512:1024].astype(F32)
    nothing = jnp.zeros((8, 64), F32)
    pieces = []
    for z in range(NZ):
        row, lane = tile_of(z)
        pieces += [total[row : row + 8, lane : lane + 64], nothing]
    rows = jnp.concatenate([firsts + seconds, jnp.concatenate(pieces, axis=0)], axis=1)
    out_ref[...] = rows.astype(BF).reshape(NZ, 16, 512)


def place(c):
    shape = (2 * BLOCK, BLOCK)
    o, s = iota(shape, 0), iota(shape, 1)
    block = (o >> 4) * NP + (o & 7)
    c = jnp.broadcast_to(c, shape)
    before = jnp.sum(jnp.where(s < block, c, 0.0), axis=1, keepdims=True)
    count = jnp.sum(jnp.where(s == block, c, 0.0), axis=1, keepdims=True)
    r = ((iota((2 * BLOCK, 1), 0) >> 3) & 1).astype(F32)
    return before + r, count > r + 0.5


def masks(c_ref, pre_ref, mask_ref):
    row, live = place(c_ref[...].astype(F32))
    pick = hot((iota((2 * BLOCK, 2 * BLOCK), 1).astype(F32) == row) & live)
    on = jnp.where(pre_ref[...].astype(F32) > 0, 1.0, 0.0).astype(BF)
    mask_ref[...] = jnp.transpose(nn(pick, on)).astype(BF)


def arrive(in_ref, c_ref, own_ref, out_ref, key_ref):
    _, live = place(c_ref[...].astype(F32))
    x = in_ref[:, :, 0:DQ].reshape(2 * BLOCK, DQ).astype(F32)
    x = jnp.where(live, x, 0.0).astype(BF)
    x = nt(eye(DQ), x).astype(BF)
    own_ref[...] = x
    out_ref[...] = jnp.broadcast_to(x[None], (NH, DQ, 2 * BLOCK))
    total = in_ref[0, 0:8, 448:512].astype(F32)
    for z in range(1, NZ):
        total = total + in_ref[z, 0:8, 448:512].astype(F32)
    key_ref[...] = jnp.concatenate([total[0:4], total[4:8]], axis=1)


def experts(rows_ref, mask_ref, wd_ref, wu_ref, out_ref):
    x = rows_ref[...].reshape(D, 2 * BLOCK)
    mid = jnp.where(mask_ref[...].astype(F32) > 0.5, nn(wd_ref[...], x), 0.0).astype(BF)
    out_ref[...] = nn(wu_ref[...], mid).astype(BF).reshape(NH, DQ, 2 * BLOCK)


def add_up(parts_ref, rows_ref, out_ref):
    total = parts_ref[0].astype(F32)
    for h in range(1, NH):
        total = total + parts_ref[h].astype(F32)
    gh = (rows_ref[...].astype(F32) + total.astype(BF).astype(F32)).astype(BF)
    out_ref[...] = jnp.broadcast_to(gh[None], (NH, DQ, 2 * BLOCK))


def combine(all_ref, recv_ref, wo_ref, out_ref):
    gh = all_ref[...].reshape(D, 2 * BLOCK)
    hg = nn(wo_ref[...], gh).astype(BF)
    q = recv_ref[:, :, DQ:448].reshape(2 * BLOCK, HD)
    a, b = halves(nn(hg, q))
    o = iota((BLOCK, 2 * BLOCK), 0)
    i = iota((BLOCK, 2 * BLOCK), 1)
    same = ((o >> 4) == (i & 7)) & ((o & 15) == (i >> 4))
    out_ref[:, :, 0:D] = nt(hot(same & ((i & 8) == 0)), gh).astype(BF).reshape(NP, 16, D)
    out_ref[:, :, D : 2 * D] = nt(hot(same & ((i & 8) != 0)), gh).astype(BF).reshape(NP, 16, D)
    out_ref[:, :, 1536:1792] = a.astype(BF)
    out_ref[:, :, 1792:2048] = b.astype(BF)


def regroup(in_ref, key_ref, out_ref):
    total = in_ref[0, :, 1536:2048].astype(F32)
    for p in range(1, NP):
        total = total + in_ref[p, :, 1536:2048].astype(F32)
    out_ref[:, :, 0:512] = jnp.broadcast_to(total.astype(BF)[None], (NZ, 16, 512))
    x = in_ref[:, :, 0:D].reshape(BLOCK, D)
    o = iota((2 * BLOCK, BLOCK), 0)
    i = iota((2 * BLOCK, BLOCK), 1)
    here = ((o & 7) == (i >> 4)) & ((o >> 4) == (i & 15))
    lower, higher = hot(here & ((o & 8) == 0)), hot(here & ((o & 8) != 0))
    rows = nn(lower, x[:, 0:384]) + nn(higher, x[:, 384:768])
    out_ref[:, :, 512:896] = rows.astype(BF).reshape(NZ, 16, 384)
    second = in_ref[0, :, D : 2 * D].astype(F32)
    for p in range(1, NP):
        second = second + in_ref[p, :, D : 2 * D].astype(F32)
    second = second.astype(BF)
    o = iota((2 * BLOCK, NZ), 0)
    i = iota((2 * BLOCK, NZ), 1)
    rows = jnp.zeros((2 * BLOCK, BLOCK), F32)
    for n in range(6):
        pick = hot(((o >> 4) == i) & ((o & 15) == n))
        rows = rows + nn(pick, second[:, n * BLOCK : (n + 1) * BLOCK])
    nothing = jnp.zeros((8, BLOCK), F32)
    key = jnp.concatenate([nothing, key_ref[...], nothing[0:4]], axis=0)
    rows = rows.reshape(NZ, 16, BLOCK) + key[None]
    out_ref[:, :, 896:1024] = rows.astype(BF)


def reduce_states(in_ref, out_ref):
    total = in_ref[0, :, 0:512].astype(F32)
    for z in range(1, NZ):
        total = total + in_ref[z, :, 0:512].astype(F32)
    upper = [None] * 8
    lower = [None] * 8
    for z in range(NZ):
        row, lane = tile_of(z)
        piece = in_ref[z, 8:16, 896:1024].astype(F32)
        piece = jnp.concatenate([piece[0:4, 0:64], piece[0:4, 64:128]], axis=0)
        (lower if row else upper)[lane // 64] = piece
    key = jnp.concatenate(
        [jnp.concatenate(upper, axis=1), jnp.concatenate(lower, axis=1)], axis=0
    )
    out_ref[:, :, 0:512] = jnp.broadcast_to(total.astype(BF)[None], (NP, 16, 512))
    out_ref[:, :, 512:1024] = jnp.broadcast_to(key.astype(BF)[None], (NP, 16, 512))


def unpack(in_ref, e_ref, wo_ref, gh_ref, hg_ref):
    e = e_ref[...]
    match, again = repeats(e)
    rank = jnp.sum(again, axis=0, keepdims=True)
    row = iota((2 * BLOCK, BLOCK), 0)
    first = ((row & 7) == (e & 7)) & ((row >> 4) == (e >> 3)) & (rank < 0.5)
    rows = in_ref[:, :, 512:896].reshape(2 * BLOCK, 384)
    second = in_ref[0, 0:8, 896:1024].astype(F32)
    for z in range(1, NZ):
        second = second + in_ref[z, 0:8, 896:1024].astype(F32)
    second = jnp.concatenate([second[n : n + 1] for n in range(6)], axis=1)
    second = jnp.broadcast_to(second, (16, D)).astype(BF)
    one = iota((16, BLOCK), 0) == 0
    gh = jnp.concatenate(
        [
            tn(hot(first & ((row & 8) == 0)), rows),
            tn(hot(first & ((row & 8) != 0)), rows),
        ],
        axis=1,
    )
    gh = (gh + tn(hot(one & (rank > 0.5)), second)).astype(BF)
    gh_ref[...] = gh
    hg_ref[...] = nt(gh, wo_ref[...]).astype(BF)


def finish(in_ref, hg_ref, k_ref, v_ref, gq_ref, gk_ref, gv_ref):
    scaling = 1.0 / math.sqrt(HD * BLOCK * BLOCK)

    def whole(at):
        a = in_ref[:, :, at : at + HD].reshape(NP, 1, 16, HD)
        b = in_ref[:, :, at + HD : at + 2 * HD].reshape(NP, 1, 16, HD)
        return jnp.concatenate([a, b], axis=1).reshape(HD, HD)

    qt, kr = whole(0), whole(512)
    gq_ref[...] = (scaling * nt(hg_ref[...], kr)).astype(BF)
    gk_ref[...] = (scaling * nn(v_ref[...], qt)).astype(BF)
    gv_ref[...] = (scaling * nt(k_ref[...], qt)).astype(BF)


def swap(tiles, axis):
    return lax.all_to_all(tiles, axis, split_axis=0, concat_axis=0, tiled=True)


def shards(out_grad, expert_of, counts, w_up, w_down, pre_act, queries, keys, values, w_out):
    e = expert_of.reshape(1, BLOCK)
    c = counts.reshape(1, BLOCK)
    rows_t = sds(NH, DQ, 2 * BLOCK)
    sent = call(pack, sds(NP, 16, 1024), e, out_grad.T, queries, keys, values, far=range(5))
    sent = call(forward, sds(NZ, 16, 512), swap(sent, PLANE))
    recv = swap(sent, "z")
    mask = call(masks, sds(D, 2 * BLOCK), c, pre_act, far=(0, 1))
    own, rows, key = call(
        arrive, [sds(DQ, 2 * BLOCK), rows_t, sds(4, BLOCK, dtype=F32)], recv, c
    )
    parts = call(experts, rows_t, swap(rows, "y"), mask, w_down[0], w_up[0])
    rows = call(add_up, rows_t, swap(parts, "y"), own)
    back = call(combine, sds(NP, 16, 2048), swap(rows, "y"), recv, w_out)
    back = call(regroup, sds(NZ, 16, 1024), swap(back, PLANE), key)
    back = swap(back, "z")
    states = swap(call(reduce_states, sds(NP, 16, 1024), back), PLANE)
    gh, hg = call(unpack, [sds(BLOCK, D), sds(BLOCK, HD)], back, e, w_out, home=1)
    outs = [sds(BLOCK, HD)] * 3
    return (gh, *call(finish, outs, states, hg, keys, values, home=3))


def solution(mesh):
    finer = Mesh(mesh.devices.reshape(16, 4, 2, mesh.shape["head"]), ("z", "x", "c", "y"))
    return jax.shard_map(
        shards,
        mesh=finer,
        in_specs=(
            P(SEQ, "y"),
            P(SEQ),
            P(None, SEQ),
            P(SEQ, None, "y"),
            P(SEQ, "y", None),
            P(SEQ, "y"),
            P(SEQ, "y"),
            P(SEQ, "y"),
            P(SEQ, "y"),
            P("y", None),
        ),
        out_specs=(P(SEQ, None), P(SEQ, "y"), P(SEQ, "y"), P(SEQ, "y")),
        check_vma=False,
    )
```

```python
import math

import jax
import jax.numpy as jnp
from jax import lax
from jax.experimental import pallas as pl
from jax.experimental.pallas import tpu as pltpu
from jax.sharding import Mesh
from jax.sharding import PartitionSpec as P

SEQ = ("z", "x", "c")
PLANE = ("x", "c")
BF, F32 = jnp.bfloat16, jnp.float32
NZ, NP, NH = 16, 8, 4
BLOCK = 128
D, HD, DQ = 768, 256, 192
LIMIT = 16 * 2**20
VMEM = pl.BlockSpec(memory_space=pltpu.VMEM)
SMEM = pl.BlockSpec(memory_space=pltpu.SMEM)


def nn(a, b):
    return lax.dot_general(a, b, (((1,), (0,)), ((), ())), preferred_element_type=F32)


def nt(a, b):
    return lax.dot_general(a, b, (((1,), (1,)), ((), ())), preferred_element_type=F32)


def tn(a, b):
    return lax.dot_general(a, b, (((0,), (0,)), ((), ())), preferred_element_type=F32)


def hot(cond):
    return jnp.where(cond, 1.0, 0.0).astype(BF)


def iota(shape, dim):
    return lax.broadcasted_iota(jnp.int32, shape, dim)


def halves(state):
    parts = state.reshape(NP, 2, 16, HD)
    return parts[:, 0], parts[:, 1]


def call(kernel, outs, *args, far=(), home=0, scalars=0):
    single = not isinstance(outs, (list, tuple))
    shapes = [outs] if single else list(outs)
    nbytes = sum(a.size * a.dtype.itemsize for a in args)

    def near(n, a):
        space = pltpu.HBM if n in far else pltpu.VMEM
        return a if n < scalars else pltpu.with_memory_space_constraint(a, space)

    res = pl.pallas_call(
        kernel,
        out_shape=[s if n < home else pltpu.VMEM(s.shape, s.dtype) for n, s in enumerate(shapes)],
        in_specs=[SMEM] * scalars + [VMEM] * (len(args) - scalars),
        out_specs=[VMEM] * len(shapes),
        cost_estimate=pl.CostEstimate(flops=10**8, bytes_accessed=nbytes, transcendentals=0),
        compiler_params=pltpu.CompilerParams(vmem_limit_bytes=LIMIT),
        name=kernel.__name__,
    )(*[near(n, a) for n, a in enumerate(args)])
    return res[0] if single else res


def sds(*shape, dtype=BF):
    return jax.ShapeDtypeStruct(shape, dtype)


def eye(n):
    return hot(iota((n, n), 0) == iota((n, n), 1))


def repeats(e):
    match = e == iota((BLOCK, BLOCK), 0)
    earlier = hot(iota((BLOCK, BLOCK), 0) < iota((BLOCK, BLOCK), 1))
    return match, jnp.where(match & (nn(hot(match), earlier) > 0.5), 1.0, 0.0)


def pack(e_ref, ogt_ref, q_ref, k_ref, v_ref, out_ref):
    match, again = repeats(e_ref[...])
    first = (jnp.where(match, 1.0, 0.0) - again).astype(BF)
    second = jnp.broadcast_to(jnp.sum(again, axis=0, keepdims=True), (16, BLOCK)).astype(BF)
    ogt, q = ogt_ref[...], q_ref[...]
    token = jnp.concatenate([nt(second, ogt), nn(second, q)], axis=1)
    spare = jnp.concatenate(
        [token[0:1, i * 64 : (i + 1) * 64] for i in range(7)] + [jnp.zeros((1, 64), F32)], axis=0
    )
    spare = jnp.broadcast_to(spare[None], (NZ, 8, 64)).reshape(BLOCK, 64)
    rows = jnp.concatenate([nt(first, ogt), nn(first, q), spare], axis=1)
    state = tn(k_ref[...], v_ref[...]).reshape(NZ, 2, 8, HD)
    state = jnp.concatenate([state[:, 0], state[:, 1]], axis=2)
    out = jnp.concatenate([rows.reshape(NZ, 8, 512), state], axis=1)
    out_ref[...] = out.astype(BF)


def forward(in_ref, out_ref, q_ref, sq_ref):
    x = in_ref[...].reshape(2 * BLOCK, 512)
    o = iota((BLOCK, 2 * BLOCK), 0)
    i = iota((BLOCK, 2 * BLOCK), 1)
    own = ((i >> 4) == (o & 15)) & ((i & 15) == (o >> 4))
    firsts = nn(hot(own), x[:, 0:448])
    q_ref[...] = firsts[:, DQ:448].astype(BF)
    spare = x[:, 448:512]
    o = iota((NZ, 2 * BLOCK), 0)
    i = iota((NZ, 2 * BLOCK), 1)
    seconds = jnp.concatenate(
        [nn(hot(((i >> 4) == o) & ((i & 15) == n)), spare) for n in range(7)], axis=1
    )
    sq_ref[...] = seconds[:, DQ:448].astype(BF)
    seconds = jnp.broadcast_to(seconds[None, :, 0:DQ], (NP, NZ, DQ)).reshape(BLOCK, DQ)
    total = in_ref[0, 8:16, :].astype(F32)
    for z in range(1, NZ):
        total = total + in_ref[z, 8:16, :].astype(F32)
    total = jnp.concatenate([total, jnp.zeros((8, 512), F32)], axis=0).astype(BF)
    o = iota((BLOCK, 16), 0)
    i = iota((BLOCK, 16), 1)
    key = jnp.zeros((BLOCK, BLOCK), F32)
    for n in range(4):
        pick = hot(((o >> 4) == i) & ((o & 15) == n))
        key = key + nn(pick, total[:, n * BLOCK : (n + 1) * BLOCK])
    rows = jnp.concatenate([firsts[:, 0:DQ], seconds, key], axis=1).astype(BF)
    rows = jnp.broadcast_to(rows.reshape(NP, 1, 16, 512), (NP, NH, 16, 512))
    out_ref[...] = rows.reshape(NP * NH, 16, 512)


def place(c):
    shape = (2 * BLOCK, BLOCK)
    o, s = iota(shape, 0), iota(shape, 1)
    block = (o & 15) * NP + ((o >> 4) & 7)
    c = jnp.broadcast_to(c, shape)
    before = jnp.sum(jnp.where(s < block, c, 0.0), axis=1, keepdims=True)
    count = jnp.sum(jnp.where(s == block, c, 0.0), axis=1, keepdims=True)
    r = (iota((2 * BLOCK, 1), 0) >> 7).astype(F32)
    return before + r, count > r + 0.5


def masks(c_ref, pre_ref, mask_ref):
    row, live = place(c_ref[...].astype(F32))
    pick = hot((iota((2 * BLOCK, 2 * BLOCK), 1).astype(F32) == row) & live)
    on = jnp.where(pre_ref[...].astype(F32) > 0, 1.0, 0.0).astype(BF)
    mask_ref[...] = jnp.transpose(nn(pick, on)).astype(BF)


def experts(h_ref, in_ref, c_ref, mask_ref, wd_ref, wu_ref, out_ref, own_ref, key_ref):
    _, live = place(c_ref[...].astype(F32))
    live = hot(live)

    def columns(h):
        x = [in_ref[p * NH + h] for p in range(NP)]
        x = jnp.concatenate(x, axis=0)
        return jnp.concatenate([x[:, 0:DQ], x[:, DQ : 2 * DQ]], axis=0) * live

    x = jnp.concatenate([columns(h) for h in range(NH)], axis=1)
    mid = jnp.where(mask_ref[...].astype(F32) > 0.5, nt(wd_ref[...], x), 0.0).astype(BF)
    out_ref[...] = nn(wu_ref[...], mid).astype(BF).reshape(NH, DQ, 2 * BLOCK)
    h = h_ref[0]
    own_ref[...] = nt(eye(DQ), columns(h)).astype(BF)
    total = in_ref[h, 0:8, 384:512].astype(F32)
    for p in range(1, NP):
        total = total + in_ref[p * NH + h, 0:8, 384:512].astype(F32)
    key_ref[...] = total[0:4]


def add_up(parts_ref, own_ref, out_ref):
    total = parts_ref[0].astype(F32)
    for h in range(1, NH):
        total = total + parts_ref[h].astype(F32)
    gh = (own_ref[...].astype(F32) + total.astype(BF).astype(F32)).astype(BF)
    rows = nt(eye(2 * BLOCK), gh)
    rows = jnp.concatenate([rows[0:BLOCK], rows[BLOCK:]], axis=1).astype(BF)
    rows = jnp.broadcast_to(rows.reshape(NP, 1, 16, 384), (NP, NH, 16, 384))
    out_ref[...] = rows.reshape(NP * NH, 16, 384)


def query_part(in_ref, q_ref, sq_ref, wo_ref, out_ref, first_ref, second_ref):
    def columns(h):
        return jnp.concatenate([in_ref[p * NH + h, :, 0:DQ] for p in range(NP)], axis=0)

    def seconds(h):
        total = in_ref[h, :, DQ : 2 * DQ].astype(F32)
        for p in range(1, NP):
            total = total + in_ref[p * NH + h, :, DQ : 2 * DQ].astype(F32)
        return total

    first = jnp.concatenate([columns(h) for h in range(NH)], axis=1)
    second = jnp.concatenate([seconds(h) for h in range(NH)], axis=1).astype(BF)
    first_ref[...] = first
    second_ref[...] = second
    wo = wo_ref[...]
    state = tn(nt(first, wo).astype(BF), q_ref[...]) + tn(nt(second, wo).astype(BF), sq_ref[...])
    a, b = halves(state)
    out_ref[:, :, 0:HD] = a.astype(BF)
    out_ref[:, :, HD:] = b.astype(BF)


def regroup(in_ref, first_ref, second_ref, key_ref, out_ref):
    total = in_ref[0].astype(F32)
    for p in range(1, NP):
        total = total + in_ref[p].astype(F32)
    out_ref[:, :, 0:512] = jnp.broadcast_to(total.astype(BF)[None], (NZ, 16, 512))
    x = first_ref[...]
    o = iota((2 * BLOCK, BLOCK), 0)
    i = iota((2 * BLOCK, BLOCK), 1)
    here = ((o & 7) == (i >> 4)) & ((o >> 4) == (i & 15))
    lower, higher = hot(here & ((o & 8) == 0)), hot(here & ((o & 8) != 0))
    rows = nn(lower, x[:, 0:384]) + nn(higher, x[:, 384:768])
    out_ref[:, :, 512:896] = rows.astype(BF).reshape(NZ, 16, 384)
    second = second_ref[...]
    o = iota((2 * BLOCK, NZ), 0)
    i = iota((2 * BLOCK, NZ), 1)
    rows = jnp.zeros((2 * BLOCK, BLOCK), F32)
    for n in range(6):
        pick = hot(((o >> 4) == i) & ((o & 15) == n))
        rows = rows + nn(pick, second[:, n * BLOCK : (n + 1) * BLOCK])
    nothing = jnp.zeros((8, BLOCK), F32)
    key = jnp.concatenate([nothing, key_ref[...], nothing[0:4]], axis=0)
    rows = rows.reshape(NZ, 16, BLOCK) + key[None]
    out_ref[:, :, 896:1024] = rows.astype(BF)


def reduce_states(in_ref, out_ref):
    total = in_ref[0, :, 0:512].astype(F32)
    for z in range(1, NZ):
        total = total + in_ref[z, :, 0:512].astype(F32)
    key = []
    for z in range(NZ):
        piece = in_ref[z, 8:16, 896:1024].astype(F32)
        key.append(jnp.concatenate([piece[n : n + 1] for n in range(4)], axis=1))
    key = jnp.concatenate(key, axis=0)
    out_ref[:, :, 0:512] = jnp.broadcast_to(total.astype(BF)[None], (NP, 16, 512))
    out_ref[:, :, 512:1024] = jnp.broadcast_to(key.astype(BF)[None], (NP, 16, 512))


def unpack(in_ref, e_ref, wo_ref, gh_ref, hg_ref):
    e = e_ref[...]
    match, again = repeats(e)
    rank = jnp.sum(again, axis=0, keepdims=True)
    row = iota((2 * BLOCK, BLOCK), 0)
    first = ((row & 7) == (e & 7)) & ((row >> 4) == (e >> 3)) & (rank < 0.5)
    rows = in_ref[:, :, 512:896].reshape(2 * BLOCK, 384)
    second = in_ref[0, 0:8, 896:1024].astype(F32)
    for z in range(1, NZ):
        second = second + in_ref[z, 0:8, 896:1024].astype(F32)
    second = jnp.concatenate([second[n : n + 1] for n in range(6)], axis=1)
    second = jnp.broadcast_to(second, (16, D)).astype(BF)
    one = iota((16, BLOCK), 0) == 0
    gh = jnp.concatenate(
        [
            tn(hot(first & ((row & 8) == 0)), rows),
            tn(hot(first & ((row & 8) != 0)), rows),
        ],
        axis=1,
    )
    gh = (gh + tn(hot(one & (rank > 0.5)), second)).astype(BF)
    gh_ref[...] = gh
    hg_ref[...] = nt(gh, wo_ref[...]).astype(BF)


def finish(in_ref, hg_ref, k_ref, v_ref, gq_ref, gk_ref, gv_ref):
    scaling = 1.0 / math.sqrt(HD * BLOCK * BLOCK)

    a = in_ref[:, :, 0:HD].reshape(NP, 1, 16, HD)
    b = in_ref[:, :, HD : 2 * HD].reshape(NP, 1, 16, HD)
    qt = jnp.concatenate([a, b], axis=1).reshape(HD, HD)
    x = in_ref[:, :, 512:1024].reshape(BLOCK, 512)
    o = iota((HD, BLOCK), 0)
    i = iota((HD, BLOCK), 1)
    same = ((i >> 4) == (o & 7)) & ((i & 15) == (o >> 4))
    kr = nn(hot(same & ((o & 8) == 0)), x[:, 0:HD]) + nn(hot(same & ((o & 8) != 0)), x[:, HD:])
    kr = kr.astype(BF)
    gq_ref[...] = (scaling * nt(hg_ref[...], kr)).astype(BF)
    gk_ref[...] = (scaling * nn(v_ref[...], qt)).astype(BF)
    gv_ref[...] = (scaling * nt(k_ref[...], qt)).astype(BF)


def swap(tiles, axis):
    return lax.all_to_all(tiles, axis, split_axis=0, concat_axis=0, tiled=True)


def shards(out_grad, expert_of, counts, w_up, w_down, pre_act, queries, keys, values, w_out):
    e = expert_of.reshape(1, BLOCK)
    c = counts.reshape(1, BLOCK)
    h = lax.axis_index("y").reshape(1)
    sent = call(pack, sds(NZ, 16, 512), e, out_grad.T, queries, keys, values, far=range(5))
    msgs, q, sq = call(
        forward, [sds(32, 16, 512), sds(BLOCK, HD), sds(NZ, HD)], swap(sent, "z")
    )
    mask = call(masks, sds(D, 2 * BLOCK), c, pre_act, far=(0, 1))
    parts, own, key = call(
        experts,
        [sds(NH, DQ, 2 * BLOCK), sds(DQ, 2 * BLOCK), sds(4, BLOCK, dtype=F32)],
        h,
        swap(msgs, PLANE + ("y",)),
        c,
        mask,
        w_down[0],
        w_up[0],
        scalars=1,
    )
    msgs = call(add_up, sds(32, 16, 384), swap(parts, "y"), own)
    msgs, first, second = call(
        query_part,
        [sds(NP, 16, 512), sds(BLOCK, D), sds(NZ, D)],
        swap(msgs, PLANE + ("y",)),
        q,
        sq,
        w_out,
    )
    back = call(regroup, sds(NZ, 16, 1024), swap(msgs, PLANE), first, second, key)
    back = swap(back, "z")
    states = swap(call(reduce_states, sds(NP, 16, 1024), back), PLANE)
    gh, hg = call(unpack, [sds(BLOCK, D), sds(BLOCK, HD)], back, e, w_out, home=1)
    outs = [sds(BLOCK, HD)] * 3
    return (gh, *call(finish, outs, states, hg, keys, values, home=3))


def solution(mesh):
    finer = Mesh(mesh.devices.reshape(16, 4, 2, mesh.shape["head"]), ("z", "x", "c", "y"))
    return jax.shard_map(
        shards,
        mesh=finer,
        in_specs=(
            P(SEQ, "y"),
            P(SEQ),
            P(None, SEQ),
            P(SEQ, None, "y"),
            P(SEQ, "y", None),
            P(SEQ, "y"),
            P(SEQ, "y"),
            P(SEQ, "y"),
            P(SEQ, "y"),
            P("y", None),
        ),
        out_specs=(P(SEQ, None), P(SEQ, "y"), P(SEQ, "y"), P(SEQ, "y")),
        check_vma=False,
    )
```

```python
import math

import jax
import jax.numpy as jnp
from jax import lax
from jax.experimental import pallas as pl
from jax.experimental.pallas import tpu as pltpu
from jax.sharding import Mesh
from jax.sharding import PartitionSpec as P

Z = ("zh", "zl")
PLANE = ("x", "c")
SEQ = Z + PLANE
BF, F32 = jnp.bfloat16, jnp.float32
NZ, NP, NH = 16, 8, 4
BLOCK = 128
D, HD, DQ = 768, 256, 192
LIMIT = 16 * 2**20
FLOPS = 10**10
VMEM = pl.BlockSpec(memory_space=pltpu.VMEM)
SMEM = pl.BlockSpec(memory_space=pltpu.SMEM)


def nn(a, b):
    return lax.dot_general(a, b, (((1,), (0,)), ((), ())), preferred_element_type=F32)


def nt(a, b):
    return lax.dot_general(a, b, (((1,), (1,)), ((), ())), preferred_element_type=F32)


def tn(a, b):
    return lax.dot_general(a, b, (((0,), (0,)), ((), ())), preferred_element_type=F32)


def hot(cond):
    return jnp.where(cond, 1.0, 0.0).astype(BF)


def iota(shape, dim):
    return lax.broadcasted_iota(jnp.int32, shape, dim)


def call(kernel, outs, *args, far=(), home=0, scalars=0):
    single = not isinstance(outs, (list, tuple))
    shapes = [outs] if single else list(outs)
    nbytes = sum(a.size * a.dtype.itemsize for a in args)

    def near(n, a):
        space = pltpu.HBM if n in far else pltpu.VMEM
        return a if n < scalars else pltpu.with_memory_space_constraint(a, space)

    res = pl.pallas_call(
        kernel,
        out_shape=[s if n < home else pltpu.VMEM(s.shape, s.dtype) for n, s in enumerate(shapes)],
        in_specs=[SMEM] * scalars + [VMEM] * (len(args) - scalars),
        out_specs=[VMEM] * len(shapes),
        cost_estimate=pl.CostEstimate(flops=FLOPS, bytes_accessed=nbytes, transcendentals=0),
        compiler_params=pltpu.CompilerParams(vmem_limit_bytes=LIMIT),
        name=kernel.__name__,
    )(*[near(n, a) for n, a in enumerate(args)])
    return res[0] if single else res


def sds(*shape, dtype=BF):
    return jax.ShapeDtypeStruct(shape, dtype)


def eye(n):
    return hot(iota((n, n), 0) == iota((n, n), 1))


def repeats(e):
    match = e == iota((BLOCK, BLOCK), 0)
    earlier = hot(iota((BLOCK, BLOCK), 0) < iota((BLOCK, BLOCK), 1))
    return match, jnp.where(match & (nn(hot(match), earlier) > 0.5), 1.0, 0.0)


def pack(_, e_ref, ogt_ref, q_ref, out_ref):
    match, again = repeats(e_ref[...])
    first = (jnp.where(match, 1.0, 0.0) - again).astype(BF)
    second = jnp.broadcast_to(jnp.sum(again, axis=0, keepdims=True), (16, BLOCK)).astype(BF)
    ogt, q = ogt_ref[...], q_ref[...]
    token = jnp.concatenate([nt(second, ogt), nn(second, q)], axis=1)
    spare = jnp.concatenate(
        [token[0:1, i * 64 : (i + 1) * 64] for i in range(7)] + [jnp.zeros((1, 64), F32)], axis=0
    )
    spare = jnp.broadcast_to(spare[None], (NZ, 8, 64)).reshape(BLOCK, 64)
    rows = jnp.concatenate([nt(first, ogt), spare], axis=1)
    out = [rows.reshape(NZ, 8, HD), nn(first, q).reshape(NZ, 8, HD)]
    out_ref[...] = jnp.concatenate(out, axis=1).astype(BF)


def forward(in_ref, out_ref, q_ref, sq_ref):
    x = in_ref[...].reshape(2 * BLOCK, HD)
    o = iota((BLOCK, 2 * BLOCK), 0)
    i = iota((BLOCK, 2 * BLOCK), 1)
    here = (i >> 4) == (o & 15)
    firsts = nn(hot(here & ((i & 15) == (o >> 4))), x[:, 0:DQ])
    q_ref[...] = nn(hot(here & ((i & 15) == (o >> 4) + 8)), x).astype(BF)
    o = iota((NZ, 2 * BLOCK), 0)
    i = iota((NZ, 2 * BLOCK), 1)
    here = (i >> 4) == o
    spare = x[:, DQ:HD]
    seconds = jnp.concatenate([nn(hot(here & ((i & 15) == n)), spare) for n in range(7)], axis=1)
    sq_ref[...] = seconds[:, DQ:448].astype(BF)
    seconds = jnp.broadcast_to(seconds[None, :, 0:DQ], (NP, NZ, DQ)).reshape(BLOCK, DQ)
    rows = jnp.concatenate([firsts, seconds], axis=1).astype(BF)
    rows = jnp.broadcast_to(rows.reshape(NP, 1, 16, 384), (NP, NH, 16, 384))
    out_ref[...] = rows.reshape(NP * NH, 16, 384)


def place(c):
    shape = (BLOCK, 2 * BLOCK)
    s, o = iota(shape, 0), iota(shape, 1)
    block = (o & 15) * NP + ((o >> 4) & 7)
    c = jnp.broadcast_to(c, (16, BLOCK)).astype(BF)
    before, count = nn(c, hot(s < block))[0:1], nn(c, hot(s == block))[0:1]
    r = (iota((1, 2 * BLOCK), 1) >> 7).astype(F32)
    return before + r, count > r + 0.5


def experts(h_ref, in_ref, c_ref, pre_ref, wd_ref, wu_ref, out_ref, own_ref):
    def columns(h):
        x = jnp.concatenate([in_ref[p * NH + h] for p in range(NP)], axis=0)
        return jnp.concatenate([x[:, 0:DQ], x[:, DQ : 2 * DQ]], axis=0)

    row, live = place(c_ref[...].astype(F32))
    pick = hot((iota((2 * BLOCK, 2 * BLOCK), 0).astype(F32) == row) & live)
    on = hot(pre_ref[...].astype(F32) > 0)
    mask = tn(on, pick)
    x = jnp.concatenate([columns(h) for h in range(NH)], axis=1)
    mid = jnp.where(mask > 0.5, nt(wd_ref[...], x), 0.0).astype(BF)
    out_ref[...] = nn(wu_ref[...], mid).astype(BF).reshape(NH, DQ, 2 * BLOCK)
    own = nt(eye(DQ), columns(h_ref[0]))
    own_ref[...] = jnp.where(live, own, 0.0).astype(BF)


def add_up(parts_ref, own_ref, out_ref):
    total = parts_ref[0].astype(F32)
    for h in range(1, NH):
        total = total + parts_ref[h].astype(F32)
    gh = (own_ref[...].astype(F32) + total.astype(BF).astype(F32)).astype(BF)
    rows = nt(eye(2 * BLOCK), gh)
    rows = jnp.concatenate([rows[0:BLOCK], rows[BLOCK:]], axis=1).astype(BF)
    rows = jnp.broadcast_to(rows.reshape(NP, 1, 16, 384), (NP, NH, 16, 384))
    out_ref[...] = rows.reshape(NP * NH, 16, 384)


def state_parts(in_ref, q_ref, sq_ref, wo_ref, k_ref, v_ref, out_ref, first_ref, second_ref):
    def columns(h):
        return jnp.concatenate([in_ref[p * NH + h, :, 0:DQ] for p in range(NP)], axis=0)

    def seconds(h):
        total = in_ref[h, :, DQ : 2 * DQ].astype(F32)
        for p in range(1, NP):
            total = total + in_ref[p * NH + h, :, DQ : 2 * DQ].astype(F32)
        return total

    first = jnp.concatenate([columns(h) for h in range(NH)], axis=1)
    second = jnp.concatenate([seconds(h) for h in range(NH)], axis=1).astype(BF)
    first_ref[...] = first
    second_ref[...] = second
    wo = wo_ref[...]
    query = tn(nt(first, wo).astype(BF), q_ref[...]) + tn(nt(second, wo).astype(BF), sq_ref[...])
    out_ref[:, :, 0:HD] = query.astype(BF).reshape(16, 16, HD)
    out_ref[:, :, HD:] = tn(k_ref[...], v_ref[...]).astype(BF).reshape(16, 16, HD)


def regroup(in_ref, first_ref, second_ref, out_ref):
    total = in_ref[0].astype(F32)
    for p in range(1, 2 * NP):
        total = total + in_ref[p].astype(F32)
    out_ref[:, :, 0:512] = jnp.broadcast_to(total.astype(BF)[None], (NZ, 16, 512))
    x = first_ref[...]
    o = iota((2 * BLOCK, BLOCK), 0)
    i = iota((2 * BLOCK, BLOCK), 1)
    here = ((o & 7) == (i >> 4)) & ((o >> 4) == (i & 15))
    lower, higher = hot(here & ((o & 8) == 0)), hot(here & ((o & 8) != 0))
    rows = nn(lower, x[:, 0:384]) + nn(higher, x[:, 384:768])
    out_ref[:, :, 512:896] = rows.astype(BF).reshape(NZ, 16, 384)
    second = second_ref[...]
    o = iota((2 * BLOCK, NZ), 0)
    i = iota((2 * BLOCK, NZ), 1)
    rows = jnp.zeros((2 * BLOCK, BLOCK), F32)
    for n in range(6):
        pick = hot(((o >> 4) == i) & ((o & 15) == n))
        rows = rows + nn(pick, second[:, n * BLOCK : (n + 1) * BLOCK])
    out_ref[:, :, 896:1024] = rows.astype(BF).reshape(NZ, 16, BLOCK)


def reduce_states(in_ref, out_ref):
    for zl in range(2):
        total = in_ref[zl, :, 0:512].astype(F32)
        for z in range(2 + zl, NZ, 2):
            total = total + in_ref[z, :, 0:512].astype(F32)
        total = jnp.broadcast_to(total.astype(BF)[None], (NP, 16, 512))
        out_ref[:, :, zl * HD : (zl + 1) * HD] = total[:, :, 0:HD]
        out_ref[:, :, 512 + zl * HD : 512 + (zl + 1) * HD] = total[:, :, HD:]


def finish(in_ref, back_ref, e_ref, wo_ref, k_ref, v_ref, gh_ref, gq_ref, gk_ref, gv_ref):
    scaling = 1.0 / math.sqrt(HD * BLOCK * BLOCK)

    def whole(at):
        a = in_ref[:, :, at : at + HD].reshape(NP, 1, 16, HD)
        b = in_ref[:, :, at + HD : at + 2 * HD].reshape(NP, 1, 16, HD)
        return jnp.concatenate([a, b], axis=1).reshape(HD, HD)

    qt, kr = whole(0), whole(512)
    e = e_ref[...]
    match, again = repeats(e)
    rank = jnp.sum(again, axis=0, keepdims=True)
    row = iota((2 * BLOCK, BLOCK), 0)
    first = ((row & 7) == (e & 7)) & ((row >> 4) == (e >> 3)) & (rank < 0.5)
    lower, higher = hot(first & ((row & 8) == 0)), hot(first & ((row & 8) != 0))
    rows = back_ref[:, :, 512:896].reshape(2 * BLOCK, 384)
    second = back_ref[0, 0:8, 896:1024].astype(F32)
    for z in range(1, NZ):
        second = second + back_ref[z, 0:8, 896:1024].astype(F32)
    second = jnp.concatenate([second[n : n + 1] for n in range(6)], axis=1)
    second = jnp.broadcast_to(second, (16, D)).astype(BF)
    one = iota((16, BLOCK), 0) == 0
    gh = jnp.concatenate([tn(lower, rows), tn(higher, rows)], axis=1)
    gh = (gh + tn(hot(one & (rank > 0.5)), second)).astype(BF)
    gh_ref[...] = gh
    hg = nt(gh, wo_ref[...]).astype(BF)
    gq_ref[...] = (scaling * nt(hg, kr)).astype(BF)
    gk_ref[...] = (scaling * nn(v_ref[...], qt)).astype(BF)
    gv_ref[...] = (scaling * nt(k_ref[...], qt)).astype(BF)


def swap(tiles, axis):
    return lax.all_to_all(tiles, axis, split_axis=0, concat_axis=0, tiled=True)


def shards(out_grad, expert_of, counts, w_up, w_down, pre_act, queries, keys, values, w_out):
    e = expert_of.reshape(1, BLOCK)
    c = counts.reshape(1, BLOCK)
    h = lax.axis_index("y").reshape(1)
    sent = call(pack, sds(NZ, 16, HD), h, e, out_grad.T, queries, far=range(1, 4), scalars=1)
    outs = [sds(32, 16, 384), sds(BLOCK, HD), sds(NZ, HD)]
    msgs, q, sq = call(forward, outs, swap(sent, Z))
    msgs = swap(msgs, PLANE + ("y",))
    outs = [sds(NH, DQ, 2 * BLOCK), sds(DQ, 2 * BLOCK)]
    parts, own = call(experts, outs, h, msgs, c, pre_act, w_down[0], w_up[0], scalars=1)
    msgs = swap(call(add_up, sds(32, 16, 384), swap(parts, "y"), own), PLANE + ("y",))
    outs = [sds(16, 16, 512), sds(BLOCK, D), sds(NZ, D)]
    msgs, first, second = call(state_parts, outs, msgs, q, sq, w_out, keys, values)
    msgs = swap(msgs, PLANE + ("zl",))
    back = swap(call(regroup, sds(NZ, 16, 1024), msgs, first, second), Z)
    states = swap(call(reduce_states, sds(NP, 16, 1024), back), PLANE)
    outs = [sds(BLOCK, D)] + [sds(BLOCK, HD)] * 3
    return tuple(call(finish, outs, states, back, e, w_out, keys, values, home=4))


def solution(mesh):
    finer = Mesh(mesh.devices.reshape(8, 2, 4, 2, mesh.shape["head"]), ("zh", "zl", "x", "c", "y"))
    return jax.shard_map(
        shards,
        mesh=finer,
        in_specs=(
            P(SEQ, "y"),
            P(SEQ),
            P(None, SEQ),
            P(SEQ, None, "y"),
            P(SEQ, "y", None),
            P(SEQ, "y"),
            P(SEQ, "y"),
            P(SEQ, "y"),
            P(SEQ, "y"),
            P("y", None),
        ),
        out_specs=(P(SEQ, None), P(SEQ, "y"), P(SEQ, "y"), P(SEQ, "y")),
        check_vma=False,
    )
```

```python
import math

import jax
import jax.numpy as jnp
from jax import lax
from jax.experimental import pallas as pl
from jax.experimental.pallas import tpu as pltpu
from jax.sharding import Mesh
from jax.sharding import PartitionSpec as P

Z = ("zh", "zl")
PLANE = ("x", "c")
SEQ = Z + PLANE
BF, F32 = jnp.bfloat16, jnp.float32
NZ, NP, NH = 16, 8, 4
BLOCK = 128
D, HD, DQ = 768, 256, 192
LIMIT = 16 * 2**20
FLOPS = 10**10
VMEM = pl.BlockSpec(memory_space=pltpu.VMEM)


def nn(a, b):
    return lax.dot_general(a, b, (((1,), (0,)), ((), ())), preferred_element_type=F32)


def nt(a, b):
    return lax.dot_general(a, b, (((1,), (1,)), ((), ())), preferred_element_type=F32)


def tn(a, b):
    return lax.dot_general(a, b, (((0,), (0,)), ((), ())), preferred_element_type=F32)


def hot(cond):
    return jnp.where(cond, 1.0, 0.0).astype(BF)


def iota(shape, dim):
    return lax.broadcasted_iota(jnp.int32, shape, dim)


def call(kernel, outs, *args, far=(), home=0):
    single = not isinstance(outs, (list, tuple))
    shapes = [outs] if single else list(outs)
    nbytes = sum(a.size * a.dtype.itemsize for a in args)

    def near(n, a):
        space = pltpu.HBM if n in far else pltpu.VMEM
        return pltpu.with_memory_space_constraint(a, space)

    res = pl.pallas_call(
        kernel,
        out_shape=[s if n < home else pltpu.VMEM(s.shape, s.dtype) for n, s in enumerate(shapes)],
        in_specs=[VMEM] * len(args),
        out_specs=[VMEM] * len(shapes),
        cost_estimate=pl.CostEstimate(flops=FLOPS, bytes_accessed=nbytes, transcendentals=0),
        compiler_params=pltpu.CompilerParams(vmem_limit_bytes=LIMIT),
        name=kernel.__name__,
    )(*[near(n, a) for n, a in enumerate(args)])
    return res[0] if single else res


def sds(*shape, dtype=BF):
    return jax.ShapeDtypeStruct(shape, dtype)


def eye(n):
    return hot(iota((n, n), 0) == iota((n, n), 1))


def repeats(e):
    match = e == iota((BLOCK, BLOCK), 0)
    earlier = hot(iota((BLOCK, BLOCK), 0) < iota((BLOCK, BLOCK), 1))
    return match, jnp.where(match & (nn(hot(match), earlier) > 0.5), 1.0, 0.0)


def pack(e_ref, ogt_ref, q_ref, out_ref):
    match, again = repeats(e_ref[...])
    first = (jnp.where(match, 1.0, 0.0) - again).astype(BF)
    second = jnp.broadcast_to(jnp.sum(again, axis=0, keepdims=True), (16, BLOCK)).astype(BF)
    ogt, q = ogt_ref[...], q_ref[...]
    token = jnp.concatenate([nt(second, ogt), nn(second, q)], axis=1)
    spare = jnp.concatenate(
        [token[0:1, i * 64 : (i + 1) * 64] for i in range(7)] + [jnp.zeros((1, 64), F32)], axis=0
    )
    spare = jnp.broadcast_to(spare[None], (NZ, 8, 64)).reshape(BLOCK, 64)
    same = hot((iota((BLOCK, BLOCK), 0) >> 3) == (iota((BLOCK, BLOCK), 1) >> 3))
    goes = jnp.broadcast_to(jnp.sum(again, axis=1, keepdims=True), (BLOCK, BLOCK)).astype(BF)
    spare = jnp.where(nn(same, goes)[:, 0:64] > 0.5, spare, 0.0)
    rows = jnp.concatenate([nt(first, ogt), spare], axis=1)
    out = [rows.reshape(NZ, 8, HD), nn(first, q).reshape(NZ, 8, HD)]
    out_ref[...] = jnp.concatenate(out, axis=1).astype(BF)


def forward(in_ref, out_ref, first_ref, second_ref, q_ref, sq_ref):
    x = in_ref[...].reshape(2 * BLOCK, HD)
    o = iota((BLOCK, 2 * BLOCK), 0)
    i = iota((BLOCK, 2 * BLOCK), 1)
    here = (i >> 4) == (o & 15)
    firsts = nn(hot(here & ((i & 15) == (o >> 4))), x[:, 0:DQ])
    first_ref[...] = firsts.astype(BF)
    q_ref[...] = nn(hot(here & ((i & 15) == (o >> 4) + 8)), x).astype(BF)
    o = iota((NZ, 2 * BLOCK), 0)
    i = iota((NZ, 2 * BLOCK), 1)
    here = (i >> 4) == o
    spare = x[:, DQ:HD]
    seconds = jnp.concatenate([nn(hot(here & ((i & 15) == n)), spare) for n in range(7)], axis=1)
    second_ref[...] = seconds[:, 0:DQ].astype(BF)
    sq_ref[...] = seconds[:, DQ:448].astype(BF)
    seconds = jnp.broadcast_to(seconds[None, :, 0:DQ], (NP, NZ, DQ)).reshape(BLOCK, DQ)
    rows = jnp.concatenate([firsts, seconds], axis=1).astype(BF)
    rows = jnp.broadcast_to(rows.reshape(NP, 1, 16, 384), (NP, NH, 16, 384))
    out_ref[...] = rows.reshape(NP * NH, 16, 384)


def place(c):
    shape = (BLOCK, 2 * BLOCK)
    s, o = iota(shape, 0), iota(shape, 1)
    block = (o & 15) * NP + ((o >> 4) & 7)
    c = jnp.broadcast_to(c, (16, BLOCK)).astype(BF)
    before, count = nn(c, hot(s < block))[0:1], nn(c, hot(s == block))[0:1]
    r = (iota((1, 2 * BLOCK), 1) >> 7).astype(F32)
    return before + r, count > r + 0.5


def experts(in_ref, c_ref, pre_ref, wd_ref, wu_ref, out_ref):
    def columns(h):
        x = jnp.concatenate([in_ref[p * NH + h] for p in range(NP)], axis=0)
        return jnp.concatenate([x[:, 0:DQ], x[:, DQ : 2 * DQ]], axis=0)

    row, live = place(c_ref[...].astype(F32))
    pick = hot((iota((2 * BLOCK, 2 * BLOCK), 0).astype(F32) == row) & live)
    mask = tn(pick, hot(pre_ref[...].astype(F32) > 0))
    x = jnp.concatenate([columns(h) for h in range(NH)], axis=1)
    mid = jnp.where(mask > 0.5, nt(x, wd_ref[...]), 0.0).astype(BF)
    part = nt(mid, wu_ref[...])
    for h in range(NH):
        own = part[:, h * DQ : (h + 1) * DQ]
        own = jnp.concatenate([own[0:BLOCK], own[BLOCK:]], axis=1).astype(BF)
        for p in range(NP):
            out_ref[p * NH + h] = own[p * 16 : (p + 1) * 16]


def add_up(in_ref, first_ref, second_ref, out_ref):
    firsts, seconds = [], jnp.zeros((16, DQ), F32)
    for p in range(NP):
        total = in_ref[p * NH].astype(F32)
        for h in range(1, NH):
            total = total + in_ref[p * NH + h].astype(F32)
        firsts.append(total[:, 0:DQ])
        seconds = seconds + total[:, DQ : 2 * DQ]

    def grad(own, added):
        return own.astype(F32) + added.astype(BF).astype(F32)

    first = grad(first_ref[...], jnp.concatenate(firsts, axis=0))
    second = grad(second_ref[...], seconds)
    rows = [
        first[:, 0:128],
        jnp.concatenate([first[0:64, 128:DQ], first[64:128, 128:DQ]], axis=1),
        second[:, 0:128],
        jnp.concatenate([second[0:8, 128:DQ], second[8:16, 128:DQ]], axis=1),
    ]
    rows = jnp.concatenate(rows, axis=0).astype(BF)
    out_ref[...] = jnp.broadcast_to(rows[None], (NH, 216, BLOCK))


def state_parts(in_ref, q_ref, sq_ref, wo_ref, k_ref, v_ref, out_ref, first_ref, second_ref):
    def columns(h):
        x = in_ref[h].astype(F32)
        last = jnp.concatenate([x[128:192, 0:64], x[128:192, 64:128]], axis=0)
        first = jnp.concatenate([x[0:128], last], axis=1)
        last = jnp.concatenate([x[208:216, 0:64], x[208:216, 64:128]], axis=0)
        return first, jnp.concatenate([x[192:208], last], axis=1)

    parts = [columns(h) for h in range(NH)]
    first = jnp.concatenate([a for a, _ in parts], axis=1).astype(BF)
    second = jnp.concatenate([b for _, b in parts], axis=1).astype(BF)
    first_ref[...] = first
    second_ref[...] = second
    wo = wo_ref[...]
    query = tn(nt(first, wo).astype(BF), q_ref[...]) + tn(nt(second, wo).astype(BF), sq_ref[...])
    out_ref[:, :, 0:HD] = query.astype(BF).reshape(16, 16, HD)
    out_ref[:, :, HD:] = tn(k_ref[...], v_ref[...]).astype(BF).reshape(16, 16, HD)


def regroup(in_ref, first_ref, second_ref, out_ref):
    total = in_ref[0].astype(F32)
    for p in range(1, 2 * NP):
        total = total + in_ref[p].astype(F32)
    out_ref[:, :, 0:512] = jnp.broadcast_to(total.astype(BF)[None], (NZ, 16, 512))
    x = first_ref[...]
    o = iota((2 * BLOCK, BLOCK), 0)
    i = iota((2 * BLOCK, BLOCK), 1)
    here = ((o & 7) == (i >> 4)) & ((o >> 4) == (i & 15))
    lower, higher = hot(here & ((o & 8) == 0)), hot(here & ((o & 8) != 0))
    rows = nn(lower, x[:, 0:384]) + nn(higher, x[:, 384:768])
    out_ref[:, :, 512:896] = rows.astype(BF).reshape(NZ, 16, 384)
    second = second_ref[...]
    o = iota((2 * BLOCK, NZ), 0)
    i = iota((2 * BLOCK, NZ), 1)
    rows = jnp.zeros((2 * BLOCK, BLOCK), F32)
    for n in range(6):
        pick = hot(((o >> 4) == i) & ((o & 15) == n))
        rows = rows + nn(pick, second[:, n * BLOCK : (n + 1) * BLOCK])
    out_ref[:, :, 896:1024] = rows.astype(BF).reshape(NZ, 16, BLOCK)


def reduce_states(in_ref, out_ref):
    for zl in range(2):
        total = in_ref[zl, :, 0:512].astype(F32)
        for z in range(2 + zl, NZ, 2):
            total = total + in_ref[z, :, 0:512].astype(F32)
        total = jnp.broadcast_to(total.astype(BF)[None], (NP, 16, 512))
        out_ref[:, :, zl * HD : (zl + 1) * HD] = total[:, :, 0:HD]
        out_ref[:, :, 512 + zl * HD : 512 + (zl + 1) * HD] = total[:, :, HD:]


def finish(in_ref, back_ref, e_ref, wo_ref, k_ref, v_ref, gh_ref, gq_ref, gk_ref, gv_ref):
    scaling = 1.0 / math.sqrt(HD * BLOCK * BLOCK)

    def whole(at):
        a = in_ref[:, :, at : at + HD].reshape(NP, 1, 16, HD)
        b = in_ref[:, :, at + HD : at + 2 * HD].reshape(NP, 1, 16, HD)
        return jnp.concatenate([a, b], axis=1).reshape(HD, HD)

    qt, kr = whole(0), whole(512)
    e = e_ref[...]
    match, again = repeats(e)
    rank = jnp.sum(again, axis=0, keepdims=True)
    row = iota((2 * BLOCK, BLOCK), 0)
    first = ((row & 7) == (e & 7)) & ((row >> 4) == (e >> 3)) & (rank < 0.5)
    lower, higher = hot(first & ((row & 8) == 0)), hot(first & ((row & 8) != 0))
    rows = back_ref[:, :, 512:896].reshape(2 * BLOCK, 384)
    second = back_ref[0, 0:8, 896:1024].astype(F32)
    for z in range(1, NZ):
        second = second + back_ref[z, 0:8, 896:1024].astype(F32)
    second = jnp.concatenate([second[n : n + 1] for n in range(6)], axis=1)
    second = jnp.broadcast_to(second, (16, D)).astype(BF)
    one = iota((16, BLOCK), 0) == 0
    gh = jnp.concatenate([tn(lower, rows), tn(higher, rows)], axis=1)
    gh = (gh + tn(hot(one & (rank > 0.5)), second)).astype(BF)
    gh_ref[...] = gh
    hg = nt(gh, wo_ref[...]).astype(BF)
    gq_ref[...] = (scaling * nt(hg, kr)).astype(BF)
    gk_ref[...] = (scaling * nn(v_ref[...], qt)).astype(BF)
    gv_ref[...] = (scaling * nt(k_ref[...], qt)).astype(BF)


def swap(tiles, axis):
    return lax.all_to_all(tiles, axis, split_axis=0, concat_axis=0, tiled=True)


def shards(out_grad, expert_of, counts, w_up, w_down, pre_act, queries, keys, values, w_out):
    e = expert_of.reshape(1, BLOCK)
    c = counts.reshape(1, BLOCK)
    sent = call(pack, sds(NZ, 16, HD), e, out_grad.T, queries, far=range(3))
    outs = [sds(32, 16, 384), sds(BLOCK, DQ), sds(NZ, DQ), sds(BLOCK, HD), sds(NZ, HD)]
    msgs, first, second, q, sq = call(forward, outs, swap(sent, Z))
    msgs = swap(msgs, PLANE + ("y",))
    msgs = call(experts, sds(32, 16, 384), msgs, c, pre_act, w_down[0], w_up[0])
    msgs = swap(msgs, PLANE + ("y",))
    msgs = swap(call(add_up, sds(NH, 216, BLOCK), msgs, first, second), "y")
    outs = [sds(16, 16, 512), sds(BLOCK, D), sds(NZ, D)]
    msgs, first, second = call(state_parts, outs, msgs, q, sq, w_out, keys, values)
    msgs = swap(msgs, PLANE + ("zl",))
    back = swap(call(regroup, sds(NZ, 16, 1024), msgs, first, second), Z)
    states = swap(call(reduce_states, sds(NP, 16, 1024), back), PLANE)
    outs = [sds(BLOCK, D)] + [sds(BLOCK, HD)] * 3
    return tuple(call(finish, outs, states, back, e, w_out, keys, values, home=4))


def solution(mesh):
    finer = Mesh(mesh.devices.reshape(8, 2, 4, 2, mesh.shape["head"]), ("zh", "zl", "x", "c", "y"))
    return jax.shard_map(
        shards,
        mesh=finer,
        in_specs=(
            P(SEQ, "y"),
            P(SEQ),
            P(None, SEQ),
            P(SEQ, None, "y"),
            P(SEQ, "y", None),
            P(SEQ, "y"),
            P(SEQ, "y"),
            P(SEQ, "y"),
            P(SEQ, "y"),
            P("y", None),
        ),
        out_specs=(P(SEQ, None), P(SEQ, "y"), P(SEQ, "y"), P(SEQ, "y")),
        check_vma=False,
    )
```

```python
import math

import jax
import jax.numpy as jnp
from jax import lax
from jax.experimental import pallas as pl
from jax.experimental.pallas import tpu as pltpu
from jax.sharding import Mesh
from jax.sharding import PartitionSpec as P

Z = ("zh", "zl")
PLANE = ("x", "c")
SEQ = Z + PLANE
BF, F32 = jnp.bfloat16, jnp.float32
NZ, NP, NH = 16, 8, 4
BLOCK = 128
D, HD, DQ = 768, 256, 192
LIMIT = 16 * 2**20
FLOPS = 10**10
VMEM = pl.BlockSpec(memory_space=pltpu.VMEM)


def nn(a, b):
    return lax.dot_general(a, b, (((1,), (0,)), ((), ())), preferred_element_type=F32)


def nt(a, b):
    return lax.dot_general(a, b, (((1,), (1,)), ((), ())), preferred_element_type=F32)


def tn(a, b):
    return lax.dot_general(a, b, (((0,), (0,)), ((), ())), preferred_element_type=F32)


def hot(cond):
    return jnp.where(cond, 1.0, 0.0).astype(BF)


def iota(shape, dim):
    return lax.broadcasted_iota(jnp.int32, shape, dim)


def call(kernel, outs, *args, far=(), home=0):
    single = not isinstance(outs, (list, tuple))
    shapes = [outs] if single else list(outs)
    nbytes = sum(a.size * a.dtype.itemsize for a in args)

    def near(n, a):
        space = pltpu.HBM if n in far else pltpu.VMEM
        return pltpu.with_memory_space_constraint(a, space)

    res = pl.pallas_call(
        kernel,
        out_shape=[s if n < home else pltpu.VMEM(s.shape, s.dtype) for n, s in enumerate(shapes)],
        in_specs=[VMEM] * len(args),
        out_specs=[VMEM] * len(shapes),
        cost_estimate=pl.CostEstimate(flops=FLOPS, bytes_accessed=nbytes, transcendentals=0),
        compiler_params=pltpu.CompilerParams(vmem_limit_bytes=LIMIT),
        name=kernel.__name__,
    )(*[near(n, a) for n, a in enumerate(args)])
    return res[0] if single else res


def sds(*shape, dtype=BF):
    return jax.ShapeDtypeStruct(shape, dtype)


def eye(n):
    return hot(iota((n, n), 0) == iota((n, n), 1))


def repeats(e):
    match = e == iota((BLOCK, BLOCK), 0)
    earlier = hot(iota((BLOCK, BLOCK), 0) < iota((BLOCK, BLOCK), 1))
    return match, jnp.where(match & (nn(hot(match), earlier) > 0.5), 1.0, 0.0)


def pack(e_ref, ogt_ref, q_ref, out_ref):
    match, again = repeats(e_ref[...])
    first = (jnp.where(match, 1.0, 0.0) - again).astype(BF)
    second = jnp.broadcast_to(jnp.sum(again, axis=0, keepdims=True), (16, BLOCK)).astype(BF)
    ogt, q = ogt_ref[...], q_ref[...]
    token = jnp.concatenate([nt(second, ogt), nn(second, q)], axis=1)
    spare = jnp.concatenate(
        [token[0:1, i * 64 : (i + 1) * 64] for i in range(7)] + [jnp.zeros((1, 64), F32)], axis=0
    )
    spare = jnp.broadcast_to(spare[None], (NZ, 8, 64)).reshape(BLOCK, 64)
    same = hot((iota((BLOCK, BLOCK), 0) >> 3) == (iota((BLOCK, BLOCK), 1) >> 3))
    goes = jnp.broadcast_to(jnp.sum(again, axis=1, keepdims=True), (BLOCK, BLOCK)).astype(BF)
    spare = jnp.where(nn(same, goes)[:, 0:64] > 0.5, spare, 0.0)
    rows = jnp.concatenate([nt(first, ogt), spare], axis=1)
    out = [rows.reshape(NZ, 8, HD), nn(first, q).reshape(NZ, 8, HD)]
    out_ref[...] = jnp.concatenate(out, axis=1).astype(BF)


def forward(in_ref, out_ref, first_ref, second_ref, q_ref, sq_ref):
    x = in_ref[...].reshape(2 * BLOCK, HD)
    o = iota((BLOCK, 2 * BLOCK), 0)
    i = iota((BLOCK, 2 * BLOCK), 1)
    here = (i >> 4) == (o & 15)
    firsts = nn(hot(here & ((i & 15) == (o >> 4))), x[:, 0:DQ])
    first_ref[...] = firsts.astype(BF)
    q_ref[...] = nn(hot(here & ((i & 15) == (o >> 4) + 8)), x).astype(BF)
    o = iota((NZ, 2 * BLOCK), 0)
    i = iota((NZ, 2 * BLOCK), 1)
    here = (i >> 4) == o
    spare = x[:, DQ:HD]
    seconds = jnp.concatenate([nn(hot(here & ((i & 15) == n)), spare) for n in range(7)], axis=1)
    second_ref[...] = seconds[:, 0:DQ].astype(BF)
    sq_ref[...] = seconds[:, DQ:448].astype(BF)
    seconds = jnp.broadcast_to(seconds[None, :, 0:DQ], (NP, NZ, DQ)).reshape(BLOCK, DQ)
    rows = jnp.concatenate([firsts, seconds], axis=1).astype(BF)
    rows = jnp.broadcast_to(rows.reshape(NP, 1, 16, 384), (NP, NH, 16, 384))
    out_ref[...] = rows.reshape(NP * NH, 16, 384)


def place(c):
    shape = (BLOCK, 2 * BLOCK)
    s, o = iota(shape, 0), iota(shape, 1)
    block = (o & 15) * NP + ((o >> 4) & 7)
    c = jnp.broadcast_to(c, (16, BLOCK)).astype(BF)
    before, count = nn(c, hot(s < block))[0:1], nn(c, hot(s == block))[0:1]
    r = (iota((1, 2 * BLOCK), 1) >> 7).astype(F32)
    return before + r, count > r + 0.5


def experts(in_ref, c_ref, pre_ref, wd_ref, wu_ref, out_ref):
    def columns(h):
        x = jnp.concatenate([in_ref[p * NH + h] for p in range(NP)], axis=0)
        return jnp.concatenate([x[:, 0:DQ], x[:, DQ : 2 * DQ]], axis=0)

    row, live = place(c_ref[...].astype(F32))
    pick = hot((iota((2 * BLOCK, 2 * BLOCK), 0).astype(F32) == row) & live)
    mask = tn(pick, hot(pre_ref[...].astype(F32) > 0))
    x = jnp.concatenate([columns(h) for h in range(NH)], axis=1)
    mid = jnp.where(mask > 0.5, nt(x, wd_ref[...]), 0.0).astype(BF)
    part = nt(mid, wu_ref[...])
    for h in range(NH):
        own = part[:, h * DQ : (h + 1) * DQ]
        own = jnp.concatenate([own[0:BLOCK], own[BLOCK:]], axis=1).astype(BF)
        for p in range(NP):
            out_ref[p * NH + h] = own[p * 16 : (p + 1) * 16]


def add_up(in_ref, first_ref, second_ref, out_ref):
    firsts, seconds = [], jnp.zeros((16, DQ), F32)
    for p in range(NP):
        total = in_ref[p * NH].astype(F32)
        for h in range(1, NH):
            total = total + in_ref[p * NH + h].astype(F32)
        firsts.append(total[:, 0:DQ])
        seconds = seconds + total[:, DQ : 2 * DQ]

    def grad(own, added):
        return own.astype(F32) + added.astype(BF).astype(F32)

    first = grad(first_ref[...], jnp.concatenate(firsts, axis=0))
    second = grad(second_ref[...], seconds)
    rows = [
        first[:, 0:128],
        jnp.concatenate([first[0:64, 128:DQ], first[64:128, 128:DQ]], axis=1),
        second[:, 0:128],
        jnp.concatenate([second[0:8, 128:DQ], second[8:16, 128:DQ]], axis=1),
    ]
    rows = jnp.concatenate(rows, axis=0).astype(BF)
    out_ref[...] = jnp.broadcast_to(rows[None], (NH, 216, BLOCK))


def state_parts(in_ref, q_ref, sq_ref, wo_ref, k_ref, v_ref, out_ref, first_ref, second_ref):
    def columns(h):
        x = in_ref[h].astype(F32)
        last = jnp.concatenate([x[128:192, 0:64], x[128:192, 64:128]], axis=0)
        first = jnp.concatenate([x[0:128], last], axis=1)
        last = jnp.concatenate([x[208:216, 0:64], x[208:216, 64:128]], axis=0)
        return first, jnp.concatenate([x[192:208], last], axis=1)

    parts = [columns(h) for h in range(NH)]
    first = jnp.concatenate([a for a, _ in parts], axis=1).astype(BF)
    second = jnp.concatenate([b for _, b in parts], axis=1).astype(BF)
    first_ref[...] = first
    second_ref[...] = second
    wo = wo_ref[...]
    query = tn(nt(first, wo).astype(BF), q_ref[...]) + tn(nt(second, wo).astype(BF), sq_ref[...])
    out_ref[:, :, 0:HD] = query.astype(BF).reshape(16, 16, HD)
    out_ref[:, :, HD:] = tn(k_ref[...], v_ref[...]).astype(BF).reshape(16, 16, HD)


def regroup(in_ref, first_ref, second_ref, out_ref):
    total = in_ref[0].astype(F32)
    for p in range(1, 2 * NP):
        total = total + in_ref[p].astype(F32)
    total = jnp.broadcast_to(total.astype(BF)[None], (NZ, 16, 512))
    for n in range(4):
        out_ref[:, n * 16 : (n + 1) * 16, :] = total[:, :, n * BLOCK : (n + 1) * BLOCK]
    x = first_ref[...]
    o = iota((2 * BLOCK, BLOCK), 0)
    i = iota((2 * BLOCK, BLOCK), 1)
    here = ((o & 7) == (i >> 4)) & ((o >> 4) == (i & 15))
    lower, higher = hot(here & ((o & 8) == 0)), hot(here & ((o & 8) != 0))
    rows = nn(lower, x[:, 0:384]) + nn(higher, x[:, 384:768])
    rows = rows.astype(BF).reshape(NZ, 16, 384)
    for n in range(3):
        out_ref[:, 64 + n * 16 : 80 + n * 16, :] = rows[:, :, n * BLOCK : (n + 1) * BLOCK]
    second = second_ref[...]
    o = iota((BLOCK, NZ), 0)
    i = iota((BLOCK, NZ), 1)
    rows = jnp.zeros((BLOCK, BLOCK), F32)
    for n in range(6):
        pick = hot(((o >> 3) == i) & ((o & 7) == n))
        rows = rows + nn(pick, second[:, n * BLOCK : (n + 1) * BLOCK])
    out_ref[:, 112:120, :] = rows.astype(BF).reshape(NZ, 8, BLOCK)


def reduce_states(in_ref, out_ref):
    for zl in range(2):
        total = in_ref[zl, 0:64, :].astype(F32)
        for z in range(2 + zl, NZ, 2):
            total = total + in_ref[z, 0:64, :].astype(F32)
        total = jnp.broadcast_to(total.astype(BF)[None], (NP, 64, BLOCK))
        for n in range(4):
            at = (n // 2) * 512 + zl * HD + (n % 2) * BLOCK
            out_ref[:, :, at : at + BLOCK] = total[:, n * 16 : (n + 1) * 16, :]


def finish(in_ref, back_ref, e_ref, wo_ref, k_ref, v_ref, gh_ref, gq_ref, gk_ref, gv_ref):
    scaling = 1.0 / math.sqrt(HD * BLOCK * BLOCK)

    def whole(at):
        a = in_ref[:, :, at : at + HD].reshape(NP, 1, 16, HD)
        b = in_ref[:, :, at + HD : at + 2 * HD].reshape(NP, 1, 16, HD)
        return jnp.concatenate([a, b], axis=1).reshape(HD, HD)

    qt, kr = whole(0), whole(512)
    e = e_ref[...]
    match, again = repeats(e)
    rank = jnp.sum(again, axis=0, keepdims=True)
    row = iota((2 * BLOCK, BLOCK), 0)
    first = ((row & 7) == (e & 7)) & ((row >> 4) == (e >> 3)) & (rank < 0.5)
    lower, higher = hot(first & ((row & 8) == 0)), hot(first & ((row & 8) != 0))
    rows = [back_ref[:, 64 + n * 16 : 80 + n * 16, :] for n in range(3)]
    rows = jnp.concatenate(rows, axis=2).reshape(2 * BLOCK, 384)
    second = back_ref[0, 112:120, :].astype(F32)
    for z in range(1, NZ):
        second = second + back_ref[z, 112:120, :].astype(F32)
    second = jnp.concatenate([second[n : n + 1] for n in range(6)], axis=1)
    second = jnp.broadcast_to(second, (16, D)).astype(BF)
    one = iota((16, BLOCK), 0) == 0
    gh = jnp.concatenate([tn(lower, rows), tn(higher, rows)], axis=1)
    gh = (gh + tn(hot(one & (rank > 0.5)), second)).astype(BF)
    gh_ref[...] = gh
    hg = nt(gh, wo_ref[...]).astype(BF)
    gq_ref[...] = (scaling * nt(hg, kr)).astype(BF)
    gk_ref[...] = (scaling * nn(v_ref[...], qt)).astype(BF)
    gv_ref[...] = (scaling * nt(k_ref[...], qt)).astype(BF)


def swap(tiles, axis):
    return lax.all_to_all(tiles, axis, split_axis=0, concat_axis=0, tiled=True)


def shards(out_grad, expert_of, counts, w_up, w_down, pre_act, queries, keys, values, w_out):
    e = expert_of.reshape(1, BLOCK)
    c = counts.reshape(1, BLOCK)
    sent = call(pack, sds(NZ, 16, HD), e, out_grad.T, queries, far=range(3))
    outs = [sds(32, 16, 384), sds(BLOCK, DQ), sds(NZ, DQ), sds(BLOCK, HD), sds(NZ, HD)]
    msgs, first, second, q, sq = call(forward, outs, swap(sent, Z))
    msgs = swap(msgs, PLANE + ("y",))
    msgs = call(experts, sds(32, 16, 384), msgs, c, pre_act, w_down[0], w_up[0])
    msgs = swap(msgs, PLANE + ("y",))
    msgs = swap(call(add_up, sds(NH, 216, BLOCK), msgs, first, second), "y")
    outs = [sds(16, 16, 512), sds(BLOCK, D), sds(NZ, D)]
    msgs, first, second = call(state_parts, outs, msgs, q, sq, w_out, keys, values)
    msgs = swap(msgs, PLANE + ("zl",))
    back = swap(call(regroup, sds(NZ, 120, BLOCK), msgs, first, second), Z)
    states = swap(call(reduce_states, sds(NP, 16, 1024), back), PLANE)
    outs = [sds(BLOCK, D)] + [sds(BLOCK, HD)] * 3
    return tuple(call(finish, outs, states, back, e, w_out, keys, values, home=4))


def solution(mesh):
    finer = Mesh(mesh.devices.reshape(8, 2, 4, 2, mesh.shape["head"]), ("zh", "zl", "x", "c", "y"))
    return jax.shard_map(
        shards,
        mesh=finer,
        in_specs=(
            P(SEQ, "y"),
            P(SEQ),
            P(None, SEQ),
            P(SEQ, None, "y"),
            P(SEQ, "y", None),
            P(SEQ, "y"),
            P(SEQ, "y"),
            P(SEQ, "y"),
            P(SEQ, "y"),
            P("y", None),
        ),
        out_specs=(P(SEQ, None), P(SEQ, "y"), P(SEQ, "y"), P(SEQ, "y")),
        check_vma=False,
    )
```

```python
import math

import jax
import jax.numpy as jnp
from jax import lax
from jax.experimental import pallas as pl
from jax.experimental.pallas import tpu as pltpu
from jax.sharding import Mesh
from jax.sharding import PartitionSpec as P

Z = ("zh", "zl")
PLANE = ("x", "c")
SEQ = Z + PLANE
BF, F32 = jnp.bfloat16, jnp.float32
NZ, NP, NH = 16, 8, 4
BLOCK = 128
D, HD, DQ = 768, 256, 192
LIMIT = 16 * 2**20
FLOPS = 10**10
VMEM = pl.BlockSpec(memory_space=pltpu.VMEM)


def nn(a, b):
    return lax.dot_general(a, b, (((1,), (0,)), ((), ())), preferred_element_type=F32)


def nt(a, b):
    return lax.dot_general(a, b, (((1,), (1,)), ((), ())), preferred_element_type=F32)


def tn(a, b):
    return lax.dot_general(a, b, (((0,), (0,)), ((), ())), preferred_element_type=F32)


def hot(cond):
    return jnp.where(cond, 1.0, 0.0).astype(BF)


def iota(shape, dim):
    return lax.broadcasted_iota(jnp.int32, shape, dim)


def call(kernel, outs, *args, far=(), home=0):
    single = not isinstance(outs, (list, tuple))
    shapes = [outs] if single else list(outs)
    nbytes = sum(a.size * a.dtype.itemsize for a in args)

    def near(n, a):
        space = pltpu.HBM if n in far else pltpu.VMEM
        return pltpu.with_memory_space_constraint(a, space)

    res = pl.pallas_call(
        kernel,
        out_shape=[s if n < home else pltpu.VMEM(s.shape, s.dtype) for n, s in enumerate(shapes)],
        in_specs=[VMEM] * len(args),
        out_specs=[VMEM] * len(shapes),
        cost_estimate=pl.CostEstimate(flops=FLOPS, bytes_accessed=nbytes, transcendentals=0),
        compiler_params=pltpu.CompilerParams(vmem_limit_bytes=LIMIT),
        name=kernel.__name__,
    )(*[near(n, a) for n, a in enumerate(args)])
    return res[0] if single else res


def sds(*shape, dtype=BF):
    return jax.ShapeDtypeStruct(shape, dtype)


def eye(n):
    return hot(iota((n, n), 0) == iota((n, n), 1))


def repeats(e):
    match = e == iota((BLOCK, BLOCK), 0)
    earlier = hot(iota((BLOCK, BLOCK), 0) < iota((BLOCK, BLOCK), 1))
    return match, jnp.where(match & (nn(hot(match), earlier) > 0.5), 1.0, 0.0)


def pack(e_ref, ogt_ref, q_ref, out_ref):
    match, again = repeats(e_ref[...])
    first = (jnp.where(match, 1.0, 0.0) - again).astype(BF)
    second = jnp.broadcast_to(jnp.sum(again, axis=0, keepdims=True), (16, BLOCK)).astype(BF)
    ogt, q = ogt_ref[...], q_ref[...]
    token = jnp.concatenate([nt(second, ogt), nn(second, q)], axis=1)
    spare = jnp.concatenate(
        [token[0:1, i * 64 : (i + 1) * 64] for i in range(7)] + [jnp.zeros((1, 64), F32)], axis=0
    )
    spare = jnp.broadcast_to(spare[None], (NZ, 8, 64)).reshape(BLOCK, 64)
    same = hot((iota((BLOCK, BLOCK), 0) >> 3) == (iota((BLOCK, BLOCK), 1) >> 3))
    goes = jnp.broadcast_to(jnp.sum(again, axis=1, keepdims=True), (BLOCK, BLOCK)).astype(BF)
    spare = jnp.where(nn(same, goes)[:, 0:64] > 0.5, spare, 0.0)
    rows = jnp.concatenate([nt(first, ogt), spare], axis=1)
    out = [rows.reshape(NZ, 8, HD), nn(first, q).reshape(NZ, 8, HD)]
    out_ref[...] = jnp.concatenate(out, axis=1).astype(BF)


def forward(in_ref, out_ref, first_ref, second_ref, q_ref, sq_ref):
    x = in_ref[...].reshape(2 * BLOCK, HD)
    o = iota((BLOCK, 2 * BLOCK), 0)
    i = iota((BLOCK, 2 * BLOCK), 1)
    here = (i >> 4) == (o & 15)
    firsts = nn(hot(here & ((i & 15) == (o >> 4))), x[:, 0:DQ])
    first_ref[...] = firsts.astype(BF)
    q_ref[...] = nn(hot(here & ((i & 15) == (o >> 4) + 8)), x).astype(BF)
    o = iota((NZ, 2 * BLOCK), 0)
    i = iota((NZ, 2 * BLOCK), 1)
    here = (i >> 4) == o
    spare = x[:, DQ:HD]
    seconds = jnp.concatenate([nn(hot(here & ((i & 15) == n)), spare) for n in range(7)], axis=1)
    second_ref[...] = seconds[:, 0:DQ].astype(BF)
    sq_ref[...] = seconds[:, DQ:448].astype(BF)
    seconds = jnp.broadcast_to(seconds[None, :, 0:DQ], (NP, NZ, DQ)).reshape(BLOCK, DQ)
    rows = jnp.concatenate([firsts, seconds], axis=1).astype(BF)
    rows = jnp.broadcast_to(rows.reshape(NP, 1, 16, 384), (NP, NH, 16, 384))
    out_ref[...] = rows.reshape(NP * NH, 16, 384)


def place(c):
    shape = (BLOCK, 2 * BLOCK)
    s, o = iota(shape, 0), iota(shape, 1)
    block = (o & 15) * NP + ((o >> 4) & 7)
    c = jnp.broadcast_to(c, (16, BLOCK)).astype(BF)
    before, count = nn(c, hot(s < block))[0:1], nn(c, hot(s == block))[0:1]
    r = (iota((1, 2 * BLOCK), 1) >> 7).astype(F32)
    return before + r, count > r + 0.5


def experts(in_ref, c_ref, pre_ref, wd_ref, wu_ref, out_ref):
    def columns(h):
        x = jnp.concatenate([in_ref[p * NH + h] for p in range(NP)], axis=0)
        return jnp.concatenate([x[:, 0:DQ], x[:, DQ : 2 * DQ]], axis=0)

    row, live = place(c_ref[...].astype(F32))
    pick = hot((iota((2 * BLOCK, 2 * BLOCK), 0).astype(F32) == row) & live)
    mask = tn(pick, hot(pre_ref[...].astype(F32) > 0))
    x = jnp.concatenate([columns(h) for h in range(NH)], axis=1)
    mid = jnp.where(mask > 0.5, nt(x, wd_ref[...]), 0.0).astype(BF)
    part = nt(mid, wu_ref[...])
    for h in range(NH):
        own = part[:, h * DQ : (h + 1) * DQ]
        own = jnp.concatenate([own[0:BLOCK], own[BLOCK:]], axis=1).astype(BF)
        for p in range(NP):
            out_ref[p * NH + h] = own[p * 16 : (p + 1) * 16]


def add_up(in_ref, first_ref, second_ref, out_ref):
    firsts, seconds = [], jnp.zeros((16, DQ), F32)
    for p in range(NP):
        total = in_ref[p * NH].astype(F32)
        for h in range(1, NH):
            total = total + in_ref[p * NH + h].astype(F32)
        firsts.append(total[:, 0:DQ])
        seconds = seconds + total[:, DQ : 2 * DQ]

    def grad(own, added):
        return own.astype(F32) + added.astype(BF).astype(F32)

    first = grad(first_ref[...], jnp.concatenate(firsts, axis=0))
    second = grad(second_ref[...], seconds)
    rows = [
        first[:, 0:128],
        jnp.concatenate([first[0:64, 128:DQ], first[64:128, 128:DQ]], axis=1),
        second[:, 0:128],
        jnp.concatenate([second[0:8, 128:DQ], second[8:16, 128:DQ]], axis=1),
    ]
    rows = jnp.concatenate(rows, axis=0).astype(BF)
    out_ref[...] = jnp.broadcast_to(rows[None], (NH, 216, BLOCK))


def state_parts(in_ref, q_ref, sq_ref, wo_ref, k_ref, v_ref, out_ref, first_ref, second_ref):
    def columns(h):
        x = in_ref[h].astype(F32)
        last = jnp.concatenate([x[128:192, 0:64], x[128:192, 64:128]], axis=0)
        first = jnp.concatenate([x[0:128], last], axis=1)
        last = jnp.concatenate([x[208:216, 0:64], x[208:216, 64:128]], axis=0)
        return first, jnp.concatenate([x[192:208], last], axis=1)

    parts = [columns(h) for h in range(NH)]
    first = jnp.concatenate([a for a, _ in parts], axis=1).astype(BF)
    second = jnp.concatenate([b for _, b in parts], axis=1).astype(BF)
    first_ref[...] = first
    second_ref[...] = second
    wo = wo_ref[...]
    query = tn(nt(first, wo).astype(BF), q_ref[...]) + tn(nt(second, wo).astype(BF), sq_ref[...])
    out_ref[:, :, 0:HD] = query.astype(BF).reshape(16, 16, HD)
    out_ref[:, :, HD:] = tn(k_ref[...], v_ref[...]).astype(BF).reshape(16, 16, HD)


def regroup(in_ref, first_ref, second_ref, out_ref):
    total = in_ref[0].astype(F32)
    for p in range(1, 2 * NP):
        total = total + in_ref[p].astype(F32)
    total = total.astype(BF)
    for z in range(NZ):
        for n in range(2):
            at = (z % 2) * HD + n * BLOCK
            out_ref[z, n * 16 : (n + 1) * 16, :] = total[:, at : at + BLOCK]
    x = first_ref[...]
    o = iota((2 * BLOCK, BLOCK), 0)
    i = iota((2 * BLOCK, BLOCK), 1)
    here = ((o & 7) == (i >> 4)) & ((o >> 4) == (i & 15))
    lower, higher = hot(here & ((o & 8) == 0)), hot(here & ((o & 8) != 0))
    rows = nn(lower, x[:, 0:384]) + nn(higher, x[:, 384:768])
    rows = rows.astype(BF).reshape(NZ, 16, 384)
    for n in range(3):
        out_ref[:, 32 + n * 16 : 48 + n * 16, :] = rows[:, :, n * BLOCK : (n + 1) * BLOCK]
    second = second_ref[...]
    o = iota((BLOCK, NZ), 0)
    i = iota((BLOCK, NZ), 1)
    rows = jnp.zeros((BLOCK, BLOCK), F32)
    for n in range(6):
        pick = hot(((o >> 3) == i) & ((o & 7) == n))
        rows = rows + nn(pick, second[:, n * BLOCK : (n + 1) * BLOCK])
    out_ref[:, 80:88, :] = rows.astype(BF).reshape(NZ, 8, BLOCK)


def reduce_states(in_ref, out_ref):
    for zl in range(2):
        total = in_ref[zl, 0:32, :].astype(F32)
        for z in range(2 + zl, NZ, 2):
            total = total + in_ref[z, 0:32, :].astype(F32)
        total = jnp.broadcast_to(total.astype(BF)[None], (2 * NP, 32, BLOCK))
        for n in range(2):
            at = zl * HD + n * BLOCK
            out_ref[:, :, at : at + BLOCK] = total[:, n * 16 : (n + 1) * 16, :]


def finish(in_ref, back_ref, e_ref, wo_ref, k_ref, v_ref, gh_ref, gq_ref, gk_ref, gv_ref):
    scaling = 1.0 / math.sqrt(HD * BLOCK * BLOCK)

    def whole(zl):
        pieces = []
        for p in range(NP):
            pieces += [in_ref[2 * p + zl, :, 0:HD], in_ref[2 * p + zl, :, HD:]]
        return jnp.concatenate(pieces, axis=0)

    qt, kr = whole(0), whole(1)
    e = e_ref[...]
    match, again = repeats(e)
    rank = jnp.sum(again, axis=0, keepdims=True)
    row = iota((2 * BLOCK, BLOCK), 0)
    first = ((row & 7) == (e & 7)) & ((row >> 4) == (e >> 3)) & (rank < 0.5)
    lower, higher = hot(first & ((row & 8) == 0)), hot(first & ((row & 8) != 0))
    rows = [back_ref[:, 32 + n * 16 : 48 + n * 16, :] for n in range(3)]
    rows = jnp.concatenate(rows, axis=2).reshape(2 * BLOCK, 384)
    second = back_ref[0, 80:88, :].astype(F32)
    for z in range(1, NZ):
        second = second + back_ref[z, 80:88, :].astype(F32)
    second = jnp.concatenate([second[n : n + 1] for n in range(6)], axis=1)
    second = jnp.broadcast_to(second, (16, D)).astype(BF)
    one = iota((16, BLOCK), 0) == 0
    gh = jnp.concatenate([tn(lower, rows), tn(higher, rows)], axis=1)
    gh = (gh + tn(hot(one & (rank > 0.5)), second)).astype(BF)
    gh_ref[...] = gh
    hg = nt(gh, wo_ref[...]).astype(BF)
    gq_ref[...] = (scaling * nt(hg, kr)).astype(BF)
    gk_ref[...] = (scaling * nn(v_ref[...], qt)).astype(BF)
    gv_ref[...] = (scaling * nt(k_ref[...], qt)).astype(BF)


def swap(tiles, axis):
    return lax.all_to_all(tiles, axis, split_axis=0, concat_axis=0, tiled=True)


def shards(out_grad, expert_of, counts, w_up, w_down, pre_act, queries, keys, values, w_out):
    e = expert_of.reshape(1, BLOCK)
    c = counts.reshape(1, BLOCK)
    sent = call(pack, sds(NZ, 16, HD), e, out_grad.T, queries, far=range(3))
    outs = [sds(32, 16, 384), sds(BLOCK, DQ), sds(NZ, DQ), sds(BLOCK, HD), sds(NZ, HD)]
    msgs, first, second, q, sq = call(forward, outs, swap(sent, Z))
    msgs = swap(msgs, PLANE + ("y",))
    msgs = call(experts, sds(32, 16, 384), msgs, c, pre_act, w_down[0], w_up[0])
    msgs = swap(msgs, PLANE + ("y",))
    msgs = swap(call(add_up, sds(NH, 216, BLOCK), msgs, first, second), "y")
    outs = [sds(16, 16, 512), sds(BLOCK, D), sds(NZ, D)]
    msgs, first, second = call(state_parts, outs, msgs, q, sq, w_out, keys, values)
    msgs = swap(msgs, PLANE + ("zl",))
    back = swap(call(regroup, sds(NZ, 88, BLOCK), msgs, first, second), Z)
    states = swap(call(reduce_states, sds(2 * NP, 16, 512), back), PLANE + ("zl",))
    outs = [sds(BLOCK, D)] + [sds(BLOCK, HD)] * 3
    return tuple(call(finish, outs, states, back, e, w_out, keys, values, home=4))


def solution(mesh):
    finer = Mesh(mesh.devices.reshape(8, 2, 4, 2, mesh.shape["head"]), ("zh", "zl", "x", "c", "y"))
    return jax.shard_map(
        shards,
        mesh=finer,
        in_specs=(
            P(SEQ, "y"),
            P(SEQ),
            P(None, SEQ),
            P(SEQ, None, "y"),
            P(SEQ, "y", None),
            P(SEQ, "y"),
            P(SEQ, "y"),
            P(SEQ, "y"),
            P(SEQ, "y"),
            P("y", None),
        ),
        out_specs=(P(SEQ, None), P(SEQ, "y"), P(SEQ, "y"), P(SEQ, "y")),
        check_vma=False,
    )
```

```python
import math

import jax
import jax.numpy as jnp
from jax import lax
from jax.experimental import pallas as pl
from jax.experimental.pallas import tpu as pltpu
from jax.sharding import Mesh
from jax.sharding import PartitionSpec as P

Z = ("zh", "zl")
PLANE = ("x", "c")
SEQ = Z + PLANE
BF, F32 = jnp.bfloat16, jnp.float32
NZ, NP, NH = 16, 8, 4
BLOCK = 128
D, HD, DQ = 768, 256, 192
LIMIT = 16 * 2**20
FLOPS = 10**10
VMEM = pl.BlockSpec(memory_space=pltpu.VMEM)


def nn(a, b):
    return lax.dot_general(a, b, (((1,), (0,)), ((), ())), preferred_element_type=F32)


def nt(a, b):
    return lax.dot_general(a, b, (((1,), (1,)), ((), ())), preferred_element_type=F32)


def tn(a, b):
    return lax.dot_general(a, b, (((0,), (0,)), ((), ())), preferred_element_type=F32)


def hot(cond):
    return jnp.where(cond, 1.0, 0.0).astype(BF)


def iota(shape, dim):
    return lax.broadcasted_iota(jnp.int32, shape, dim)


def call(kernel, outs, *args, far=(), home=0):
    single = not isinstance(outs, (list, tuple))
    shapes = [outs] if single else list(outs)
    nbytes = sum(a.size * a.dtype.itemsize for a in args)

    def near(n, a):
        space = pltpu.HBM if n in far else pltpu.VMEM
        return pltpu.with_memory_space_constraint(a, space)

    res = pl.pallas_call(
        kernel,
        out_shape=[s if n < home else pltpu.VMEM(s.shape, s.dtype) for n, s in enumerate(shapes)],
        in_specs=[VMEM] * len(args),
        out_specs=[VMEM] * len(shapes),
        cost_estimate=pl.CostEstimate(flops=FLOPS, bytes_accessed=nbytes, transcendentals=0),
        compiler_params=pltpu.CompilerParams(vmem_limit_bytes=LIMIT),
        name=kernel.__name__,
    )(*[near(n, a) for n, a in enumerate(args)])
    return res[0] if single else res


def sds(*shape, dtype=BF):
    return jax.ShapeDtypeStruct(shape, dtype)


def eye(n):
    return hot(iota((n, n), 0) == iota((n, n), 1))


def repeats(e):
    match = e == iota((BLOCK, BLOCK), 0)
    earlier = hot(iota((BLOCK, BLOCK), 0) < iota((BLOCK, BLOCK), 1))
    return match, jnp.where(match & (nn(hot(match), earlier) > 0.5), 1.0, 0.0)


def pack(e_ref, ogt_ref, q_ref, out_ref):
    match, again = repeats(e_ref[...])
    first = (jnp.where(match, 1.0, 0.0) - again).astype(BF)
    second = jnp.broadcast_to(jnp.sum(again, axis=0, keepdims=True), (16, BLOCK)).astype(BF)
    ogt, q = ogt_ref[...], q_ref[...]
    token = jnp.concatenate([nt(second, ogt), nn(second, q)], axis=1)
    spare = jnp.concatenate(
        [token[0:1, i * 64 : (i + 1) * 64] for i in range(7)] + [jnp.zeros((1, 64), F32)], axis=0
    )
    spare = jnp.broadcast_to(spare[None], (NZ, 8, 64)).reshape(BLOCK, 64)
    same = hot((iota((BLOCK, BLOCK), 0) >> 3) == (iota((BLOCK, BLOCK), 1) >> 3))
    goes = jnp.broadcast_to(jnp.sum(again, axis=1, keepdims=True), (BLOCK, BLOCK)).astype(BF)
    spare = jnp.where(nn(same, goes)[:, 0:64] > 0.5, spare, 0.0)
    rows = jnp.concatenate([nt(first, ogt), spare], axis=1)
    out = [rows.reshape(NZ, 8, HD), nn(first, q).reshape(NZ, 8, HD)]
    out_ref[...] = jnp.concatenate(out, axis=1).astype(BF)


def forward(in_ref, out_ref, first_ref, second_ref, q_ref, sq_ref):
    x = in_ref[...].reshape(2 * BLOCK, HD)
    o = iota((BLOCK, 2 * BLOCK), 0)
    i = iota((BLOCK, 2 * BLOCK), 1)
    here = (i >> 4) == (o & 15)
    firsts = nn(hot(here & ((i & 15) == (o >> 4))), x[:, 0:DQ])
    first_ref[...] = firsts.astype(BF)
    q_ref[...] = nn(hot(here & ((i & 15) == (o >> 4) + 8)), x).astype(BF)
    o = iota((NZ, 2 * BLOCK), 0)
    i = iota((NZ, 2 * BLOCK), 1)
    here = (i >> 4) == o
    spare = x[:, DQ:HD]
    seconds = jnp.concatenate([nn(hot(here & ((i & 15) == n)), spare) for n in range(7)], axis=1)
    second_ref[...] = seconds[:, 0:DQ].astype(BF)
    sq_ref[...] = seconds[:, DQ:448].astype(BF)
    seconds = jnp.broadcast_to(seconds[None, :, 0:DQ], (NP, NZ, DQ)).reshape(BLOCK, DQ)
    rows = jnp.concatenate([firsts, seconds], axis=1).astype(BF)
    rows = jnp.broadcast_to(rows.reshape(NP, 1, 16, 384), (NP, NH, 16, 384))
    out_ref[...] = rows.reshape(NP * NH, 16, 384)


def place(c):
    shape = (BLOCK, 2 * BLOCK)
    s, o = iota(shape, 0), iota(shape, 1)
    block = (o & 15) * NP + ((o >> 4) & 7)
    c = jnp.broadcast_to(c, (16, BLOCK)).astype(BF)
    before, count = nn(c, hot(s < block))[0:1], nn(c, hot(s == block))[0:1]
    r = (iota((1, 2 * BLOCK), 1) >> 7).astype(F32)
    return before + r, count > r + 0.5


def experts(in_ref, c_ref, pre_ref, wd_ref, wu_ref, out_ref):
    def columns(h):
        x = jnp.concatenate([in_ref[p * NH + h] for p in range(NP)], axis=0)
        return jnp.concatenate([x[:, 0:DQ], x[:, DQ : 2 * DQ]], axis=0)

    row, live = place(c_ref[...].astype(F32))
    pick = hot((iota((2 * BLOCK, 2 * BLOCK), 0).astype(F32) == row) & live)
    mask = tn(pick, hot(pre_ref[...].astype(F32) > 0))
    x = jnp.concatenate([columns(h) for h in range(NH)], axis=1)
    mid = jnp.where(mask > 0.5, nt(x, wd_ref[...]), 0.0).astype(BF)
    part = nt(mid, wu_ref[...])
    for h in range(NH):
        own = part[:, h * DQ : (h + 1) * DQ]
        own = jnp.concatenate([own[0:BLOCK], own[BLOCK:]], axis=1).astype(BF)
        for p in range(NP):
            out_ref[p * NH + h] = own[p * 16 : (p + 1) * 16]


def add_up(in_ref, first_ref, second_ref, out_ref):
    firsts, seconds = [], jnp.zeros((16, DQ), F32)
    for p in range(NP):
        total = in_ref[p * NH].astype(F32)
        for h in range(1, NH):
            total = total + in_ref[p * NH + h].astype(F32)
        firsts.append(total[:, 0:DQ])
        seconds = seconds + total[:, DQ : 2 * DQ]

    def grad(own, added):
        return own.astype(F32) + added.astype(BF).astype(F32)

    first = grad(first_ref[...], jnp.concatenate(firsts, axis=0))
    second = grad(second_ref[...], seconds)
    rows = [
        first[:, 0:128],
        jnp.concatenate([first[0:64, 128:DQ], first[64:128, 128:DQ]], axis=1),
        second[:, 0:128],
        jnp.concatenate([second[0:8, 128:DQ], second[8:16, 128:DQ]], axis=1),
    ]
    rows = jnp.concatenate(rows, axis=0).astype(BF)
    out_ref[...] = jnp.broadcast_to(rows[None], (NH, 216, BLOCK))


def state_parts(in_ref, q_ref, sq_ref, wo_ref, k_ref, v_ref, out_ref, first_ref, second_ref):
    def columns(h):
        x = in_ref[h].astype(F32)
        last = jnp.concatenate([x[128:192, 0:64], x[128:192, 64:128]], axis=0)
        first = jnp.concatenate([x[0:128], last], axis=1)
        last = jnp.concatenate([x[208:216, 0:64], x[208:216, 64:128]], axis=0)
        return first, jnp.concatenate([x[192:208], last], axis=1)

    parts = [columns(h) for h in range(NH)]
    first = jnp.concatenate([a for a, _ in parts], axis=1).astype(BF)
    second = jnp.concatenate([b for _, b in parts], axis=1).astype(BF)
    first_ref[...] = first
    second_ref[...] = second
    wo = wo_ref[...]
    query = tn(nt(first, wo).astype(BF), q_ref[...]) + tn(nt(second, wo).astype(BF), sq_ref[...])
    out_ref[:, :, 0:HD] = query.astype(BF).reshape(16, 16, HD)
    out_ref[:, :, HD:] = tn(k_ref[...], v_ref[...]).astype(BF).reshape(16, 16, HD)


def regroup(in_ref, first_ref, second_ref, out_ref):
    total = in_ref[0].astype(F32)
    for p in range(1, 2 * NP):
        total = total + in_ref[p].astype(F32)
    total = total.astype(BF)
    for z in range(NZ):
        for n in range(2):
            at = (z % 2) * HD + n * BLOCK
            out_ref[z, n * 16 : (n + 1) * 16, :] = total[:, at : at + BLOCK]
    x = first_ref[...]
    o = iota((2 * BLOCK, BLOCK), 0)
    i = iota((2 * BLOCK, BLOCK), 1)
    here = ((o & 7) == (i >> 4)) & ((o >> 4) == (i & 15))
    lower, higher = hot(here & ((o & 8) == 0)), hot(here & ((o & 8) != 0))
    rows = nn(lower, x[:, 0:384]) + nn(higher, x[:, 384:768])
    rows = rows.astype(BF).reshape(NZ, 16, 384)
    for n in range(3):
        out_ref[:, 32 + n * 16 : 48 + n * 16, :] = rows[:, :, n * BLOCK : (n + 1) * BLOCK]
    second = second_ref[...]
    o = iota((BLOCK, NZ), 0)
    i = iota((BLOCK, NZ), 1)
    rows = jnp.zeros((BLOCK, BLOCK), F32)
    for n in range(6):
        pick = hot(((o >> 3) == i) & ((o & 7) == n))
        rows = rows + nn(pick, second[:, n * BLOCK : (n + 1) * BLOCK])
    out_ref[:, 80:88, :] = rows.astype(BF).reshape(NZ, 8, BLOCK)


def reduce_states(in_ref, out_ref):
    for zl in range(2):
        total = in_ref[zl, 0:32, :].astype(F32)
        for z in range(2 + zl, NZ, 2):
            total = total + in_ref[z, 0:32, :].astype(F32)
        total = jnp.broadcast_to(total.astype(BF)[None], (2 * NP, 32, BLOCK))
        for n in range(2):
            at = zl * HD + n * BLOCK
            out_ref[:, :, at : at + BLOCK] = total[:, n * 16 : (n + 1) * 16, :]


def finish(in_ref, back_ref, e_ref, wo_ref, k_ref, v_ref, gh_ref, gq_ref, gk_ref, gv_ref):
    scaling = 1.0 / math.sqrt(HD * BLOCK * BLOCK)

    def whole(zl):
        pieces = []
        for p in range(NP):
            pieces += [in_ref[2 * p + zl, :, 0:HD], in_ref[2 * p + zl, :, HD:]]
        return jnp.concatenate(pieces, axis=0)

    qt, kr = whole(0), whole(1)
    match, again = repeats(e_ref[...])
    rank = jnp.sum(again, axis=0, keepdims=True)
    first = (jnp.where(match, 1.0, 0.0) - again).astype(BF)
    rows = [back_ref[:, 32 + n * 16 : 48 + n * 16, :] for n in range(3)]
    rows = jnp.concatenate(rows, axis=2).astype(F32)
    lower = rows[:, 0:8].reshape(BLOCK, 384).astype(BF)
    higher = rows[:, 8:16].reshape(BLOCK, 384).astype(BF)
    second = back_ref[0, 80:88, :].astype(F32)
    for z in range(1, NZ):
        second = second + back_ref[z, 80:88, :].astype(F32)
    second = jnp.concatenate([second[n : n + 1] for n in range(6)], axis=1)
    second = jnp.broadcast_to(second, (16, D)).astype(BF)
    one = iota((16, BLOCK), 0) == 0
    gh = jnp.concatenate([tn(first, lower), tn(first, higher)], axis=1)
    gh = (gh + tn(hot(one & (rank > 0.5)), second)).astype(BF)
    gh_ref[...] = gh
    hg = nt(gh, wo_ref[...]).astype(BF)
    gq_ref[...] = (scaling * nt(hg, kr)).astype(BF)
    gk_ref[...] = (scaling * nn(v_ref[...], qt)).astype(BF)
    gv_ref[...] = (scaling * nt(k_ref[...], qt)).astype(BF)


def swap(tiles, axis):
    return lax.all_to_all(tiles, axis, split_axis=0, concat_axis=0, tiled=True)


def shards(out_grad, expert_of, counts, w_up, w_down, pre_act, queries, keys, values, w_out):
    e = expert_of.reshape(1, BLOCK)
    c = counts.reshape(1, BLOCK)
    sent = call(pack, sds(NZ, 16, HD), e, out_grad.T, queries, far=range(3))
    outs = [sds(32, 16, 384), sds(BLOCK, DQ), sds(NZ, DQ), sds(BLOCK, HD), sds(NZ, HD)]
    msgs, first, second, q, sq = call(forward, outs, swap(sent, Z))
    msgs = swap(msgs, PLANE + ("y",))
    msgs = call(experts, sds(32, 16, 384), msgs, c, pre_act, w_down[0], w_up[0])
    msgs = swap(msgs, PLANE + ("y",))
    msgs = swap(call(add_up, sds(NH, 216, BLOCK), msgs, first, second), "y")
    outs = [sds(16, 16, 512), sds(BLOCK, D), sds(NZ, D)]
    msgs, first, second = call(state_parts, outs, msgs, q, sq, w_out, keys, values)
    msgs = swap(msgs, PLANE + ("zl",))
    back = swap(call(regroup, sds(NZ, 88, BLOCK), msgs, first, second), Z)
    states = swap(call(reduce_states, sds(2 * NP, 16, 512), back), PLANE + ("zl",))
    outs = [sds(BLOCK, D)] + [sds(BLOCK, HD)] * 3
    return tuple(call(finish, outs, states, back, e, w_out, keys, values, home=4))


def solution(mesh):
    finer = Mesh(mesh.devices.reshape(8, 2, 4, 2, mesh.shape["head"]), ("zh", "zl", "x", "c", "y"))
    return jax.shard_map(
        shards,
        mesh=finer,
        in_specs=(
            P(SEQ, "y"),
            P(SEQ),
            P(None, SEQ),
            P(SEQ, None, "y"),
            P(SEQ, "y", None),
            P(SEQ, "y"),
            P(SEQ, "y"),
            P(SEQ, "y"),
            P(SEQ, "y"),
            P("y", None),
        ),
        out_specs=(P(SEQ, None), P(SEQ, "y"), P(SEQ, "y"), P(SEQ, "y")),
        check_vma=False,
    )
```

```python
import math

import jax
import jax.numpy as jnp
from jax import lax
from jax.experimental import pallas as pl
from jax.experimental.pallas import tpu as pltpu
from jax.sharding import Mesh
from jax.sharding import PartitionSpec as P

Z = ("zh", "zl")
PLANE = ("x", "c")
SEQ = Z + PLANE
BF, F32 = jnp.bfloat16, jnp.float32
NZ, NP, NH = 16, 8, 4
BLOCK = 128
D, HD, DQ = 768, 256, 192
LIMIT = 16 * 2**20
FLOPS = 10**10
VMEM = pl.BlockSpec(memory_space=pltpu.VMEM)


def nn(a, b):
    return lax.dot_general(a, b, (((1,), (0,)), ((), ())), preferred_element_type=F32)


def nt(a, b):
    return lax.dot_general(a, b, (((1,), (1,)), ((), ())), preferred_element_type=F32)


def tn(a, b):
    return lax.dot_general(a, b, (((0,), (0,)), ((), ())), preferred_element_type=F32)


def hot(cond):
    return jnp.where(cond, 1.0, 0.0).astype(BF)


def iota(shape, dim):
    return lax.broadcasted_iota(jnp.int32, shape, dim)


def call(kernel, outs, *args, far=(), home=0):
    single = not isinstance(outs, (list, tuple))
    shapes = [outs] if single else list(outs)
    nbytes = sum(a.size * a.dtype.itemsize for a in args)

    def near(n, a):
        space = pltpu.HBM if n in far else pltpu.VMEM
        return pltpu.with_memory_space_constraint(a, space)

    res = pl.pallas_call(
        kernel,
        out_shape=[s if n < home else pltpu.VMEM(s.shape, s.dtype) for n, s in enumerate(shapes)],
        in_specs=[VMEM] * len(args),
        out_specs=[VMEM] * len(shapes),
        cost_estimate=pl.CostEstimate(flops=FLOPS, bytes_accessed=nbytes, transcendentals=0),
        compiler_params=pltpu.CompilerParams(vmem_limit_bytes=LIMIT),
        name=kernel.__name__,
    )(*[near(n, a) for n, a in enumerate(args)])
    return res[0] if single else res


def sds(*shape, dtype=BF):
    return jax.ShapeDtypeStruct(shape, dtype)


def eye(n):
    return hot(iota((n, n), 0) == iota((n, n), 1))


def repeats(e):
    match = e == iota((BLOCK, BLOCK), 0)
    earlier = hot(iota((BLOCK, BLOCK), 0) < iota((BLOCK, BLOCK), 1))
    return match, jnp.where(match & (nn(hot(match), earlier) > 0.5), 1.0, 0.0)


def pack(e_ref, ogt_ref, q_ref, out_ref):
    match, again = repeats(e_ref[...])
    first = (jnp.where(match, 1.0, 0.0) - again).astype(BF)
    second = jnp.broadcast_to(jnp.sum(again, axis=0, keepdims=True), (16, BLOCK)).astype(BF)
    ogt, q = ogt_ref[...], q_ref[...]
    token = jnp.concatenate([nt(second, ogt), nn(second, q)], axis=1)
    spare = jnp.concatenate(
        [token[0:1, i * 64 : (i + 1) * 64] for i in range(7)] + [jnp.zeros((1, 64), F32)], axis=0
    )
    spare = jnp.broadcast_to(spare[None], (NZ, 8, 64)).reshape(BLOCK, 64)
    same = hot((iota((BLOCK, BLOCK), 0) >> 3) == (iota((BLOCK, BLOCK), 1) >> 3))
    goes = jnp.broadcast_to(jnp.sum(again, axis=1, keepdims=True), (BLOCK, BLOCK)).astype(BF)
    spare = jnp.where(nn(same, goes)[:, 0:64] > 0.5, spare, 0.0)
    rows = jnp.concatenate([nt(first, ogt), spare], axis=1)
    out = [rows.reshape(NZ, 8, HD), nn(first, q).reshape(NZ, 8, HD)]
    out_ref[...] = jnp.concatenate(out, axis=1).astype(BF)


def forward(in_ref, out_ref, first_ref, second_ref, q_ref, sq_ref):
    x = in_ref[...].reshape(2 * BLOCK, HD)
    o = iota((BLOCK, 2 * BLOCK), 0)
    i = iota((BLOCK, 2 * BLOCK), 1)
    here = (i >> 4) == (o & 15)
    firsts = nn(hot(here & ((i & 15) == (o >> 4))), x[:, 0:DQ])
    first_ref[...] = firsts.astype(BF)
    q_ref[...] = nn(hot(here & ((i & 15) == (o >> 4) + 8)), x).astype(BF)
    o = iota((NZ, 2 * BLOCK), 0)
    i = iota((NZ, 2 * BLOCK), 1)
    here = (i >> 4) == o
    spare = x[:, DQ:HD]
    seconds = jnp.concatenate([nn(hot(here & ((i & 15) == n)), spare) for n in range(7)], axis=1)
    second_ref[...] = seconds[:, 0:DQ].astype(BF)
    sq_ref[...] = seconds[:, DQ:448].astype(BF)
    seconds = jnp.broadcast_to(seconds[None, :, 0:DQ], (NP, NZ, DQ)).reshape(BLOCK, DQ)
    rows = jnp.concatenate([firsts, seconds], axis=1).astype(BF)
    rows = jnp.broadcast_to(rows.reshape(NP, 1, 16, 384), (NP, NH, 16, 384))
    out_ref[...] = rows.reshape(NP * NH, 16, 384)


def place(c):
    shape = (BLOCK, 2 * BLOCK)
    s, o = iota(shape, 0), iota(shape, 1)
    block = (o & 15) * NP + ((o >> 4) & 7)
    c = jnp.broadcast_to(c, (16, BLOCK)).astype(BF)
    before, count = nn(c, hot(s < block))[0:1], nn(c, hot(s == block))[0:1]
    r = (iota((1, 2 * BLOCK), 1) >> 7).astype(F32)
    return before + r, count > r + 0.5


def experts(in_ref, c_ref, pre_ref, wd_ref, wu_ref, out_ref):
    def columns(h):
        x = jnp.concatenate([in_ref[p * NH + h] for p in range(NP)], axis=0)
        return jnp.concatenate([x[:, 0:DQ], x[:, DQ : 2 * DQ]], axis=0)

    row, live = place(c_ref[...].astype(F32))
    pick = hot((iota((2 * BLOCK, 2 * BLOCK), 0).astype(F32) == row) & live)
    mask = tn(pick, hot(pre_ref[...].astype(F32) > 0))
    x = jnp.concatenate([columns(h) for h in range(NH)], axis=1)
    mid = jnp.where(mask > 0.5, nt(x, wd_ref[...]), 0.0).astype(BF)
    part = nt(mid, wu_ref[...])
    for h in range(NH):
        own = part[:, h * DQ : (h + 1) * DQ]
        own = jnp.concatenate([own[0:BLOCK], own[BLOCK:]], axis=1).astype(BF)
        for p in range(NP):
            out_ref[p * NH + h] = own[p * 16 : (p + 1) * 16]


def add_up(in_ref, first_ref, second_ref, out_ref):
    firsts, seconds = [], jnp.zeros((16, DQ), F32)
    for p in range(NP):
        total = in_ref[p * NH].astype(F32)
        for h in range(1, NH):
            total = total + in_ref[p * NH + h].astype(F32)
        firsts.append(total[:, 0:DQ])
        seconds = seconds + total[:, DQ : 2 * DQ]

    def grad(own, added):
        return own.astype(F32) + added.astype(BF).astype(F32)

    first = grad(first_ref[...], jnp.concatenate(firsts, axis=0))
    second = grad(second_ref[...], seconds)
    rows = [
        first[:, 0:128],
        jnp.concatenate([first[0:64, 128:DQ], first[64:128, 128:DQ]], axis=1),
        second[:, 0:128],
        jnp.concatenate([second[0:8, 128:DQ], second[8:16, 128:DQ]], axis=1),
    ]
    rows = jnp.concatenate(rows, axis=0).astype(BF)
    out_ref[...] = jnp.broadcast_to(rows[None], (NH, 216, BLOCK))


def state_parts(in_ref, q_ref, sq_ref, wo_ref, k_ref, v_ref, out_ref, first_ref, second_ref):
    def columns(h):
        x = in_ref[h].astype(F32)
        last = jnp.concatenate([x[128:192, 0:64], x[128:192, 64:128]], axis=0)
        first = jnp.concatenate([x[0:128], last], axis=1)
        last = jnp.concatenate([x[208:216, 0:64], x[208:216, 64:128]], axis=0)
        return first, jnp.concatenate([x[192:208], last], axis=1)

    parts = [columns(h) for h in range(NH)]
    first = jnp.concatenate([a for a, _ in parts], axis=1).astype(BF)
    second = jnp.concatenate([b for _, b in parts], axis=1).astype(BF)
    first_ref[...] = first
    second_ref[...] = second
    wo = wo_ref[...]
    query = tn(nt(first, wo).astype(BF), q_ref[...]) + tn(nt(second, wo).astype(BF), sq_ref[...])
    query = query.astype(BF).reshape(NP, 2, 16, HD)
    key = tn(k_ref[...], v_ref[...]).astype(BF).reshape(NP, 2, 16, HD)
    for zl in range(2):
        out_ref[zl * NP : (zl + 1) * NP, :, 0:HD] = query[:, zl]
        out_ref[zl * NP : (zl + 1) * NP, :, HD:] = key[:, zl]


def regroup(in_ref, first_ref, second_ref, out_ref):
    total = in_ref[0].astype(F32)
    for p in range(1, 2 * NP):
        total = total + in_ref[p].astype(F32)
    total = total.astype(BF)
    for z in range(NZ):
        for n in range(2):
            at = (z % 2) * HD + n * BLOCK
            out_ref[z, n * 16 : (n + 1) * 16, :] = total[:, at : at + BLOCK]
    x = first_ref[...]
    o = iota((2 * BLOCK, BLOCK), 0)
    i = iota((2 * BLOCK, BLOCK), 1)
    here = ((o & 7) == (i >> 4)) & ((o >> 4) == (i & 15))
    lower, higher = hot(here & ((o & 8) == 0)), hot(here & ((o & 8) != 0))
    rows = nn(lower, x[:, 0:384]) + nn(higher, x[:, 384:768])
    rows = rows.astype(BF).reshape(NZ, 16, 384)
    for n in range(3):
        out_ref[:, 32 + n * 16 : 48 + n * 16, :] = rows[:, :, n * BLOCK : (n + 1) * BLOCK]
    second = second_ref[...]
    o = iota((BLOCK, NZ), 0)
    i = iota((BLOCK, NZ), 1)
    rows = jnp.zeros((BLOCK, BLOCK), F32)
    for n in range(6):
        pick = hot(((o >> 3) == i) & ((o & 7) == n))
        rows = rows + nn(pick, second[:, n * BLOCK : (n + 1) * BLOCK])
    out_ref[:, 80:88, :] = rows.astype(BF).reshape(NZ, 8, BLOCK)


def reduce_states(in_ref, out_ref):
    for zl in range(2):
        total = in_ref[zl, 0:32, :].astype(F32)
        for z in range(2 + zl, NZ, 2):
            total = total + in_ref[z, 0:32, :].astype(F32)
        total = jnp.broadcast_to(total.astype(BF)[None], (2 * NP, 32, BLOCK))
        for n in range(2):
            at = zl * HD + n * BLOCK
            out_ref[:, :, at : at + BLOCK] = total[:, n * 16 : (n + 1) * 16, :]


def finish(in_ref, back_ref, e_ref, wo_ref, k_ref, v_ref, gh_ref, gq_ref, gk_ref, gv_ref):
    scaling = 1.0 / math.sqrt(HD * BLOCK * BLOCK)

    def whole(zl):
        pieces = []
        for p in range(NP):
            pieces += [in_ref[zl * NP + p, :, 0:HD], in_ref[zl * NP + p, :, HD:]]
        return jnp.concatenate(pieces, axis=0)

    qt, kr = whole(0), whole(1)
    match, again = repeats(e_ref[...])
    rank = jnp.sum(again, axis=0, keepdims=True)
    first = (jnp.where(match, 1.0, 0.0) - again).astype(BF)
    rows = [back_ref[:, 32 + n * 16 : 48 + n * 16, :] for n in range(3)]
    rows = jnp.concatenate(rows, axis=2).astype(F32)
    lower = rows[:, 0:8].reshape(BLOCK, 384).astype(BF)
    higher = rows[:, 8:16].reshape(BLOCK, 384).astype(BF)
    second = back_ref[0, 80:88, :].astype(F32)
    for z in range(1, NZ):
        second = second + back_ref[z, 80:88, :].astype(F32)
    second = jnp.concatenate([second[n : n + 1] for n in range(6)], axis=1)
    second = jnp.broadcast_to(second, (16, D)).astype(BF)
    one = iota((16, BLOCK), 0) == 0
    gh = jnp.concatenate([tn(first, lower), tn(first, higher)], axis=1)
    gh = (gh + tn(hot(one & (rank > 0.5)), second)).astype(BF)
    gh_ref[...] = gh
    hg = nt(gh, wo_ref[...]).astype(BF)
    gq_ref[...] = (scaling * nt(hg, kr)).astype(BF)
    gk_ref[...] = (scaling * nn(v_ref[...], qt)).astype(BF)
    gv_ref[...] = (scaling * nt(k_ref[...], qt)).astype(BF)


def swap(tiles, axis):
    return lax.all_to_all(tiles, axis, split_axis=0, concat_axis=0, tiled=True)


def shards(out_grad, expert_of, counts, w_up, w_down, pre_act, queries, keys, values, w_out):
    e = expert_of.reshape(1, BLOCK)
    c = counts.reshape(1, BLOCK)
    sent = call(pack, sds(NZ, 16, HD), e, out_grad.T, queries, far=range(3))
    outs = [sds(32, 16, 384), sds(BLOCK, DQ), sds(NZ, DQ), sds(BLOCK, HD), sds(NZ, HD)]
    msgs, first, second, q, sq = call(forward, outs, swap(sent, Z))
    msgs = swap(msgs, PLANE + ("y",))
    msgs = call(experts, sds(32, 16, 384), msgs, c, pre_act, w_down[0], w_up[0])
    msgs = swap(msgs, PLANE + ("y",))
    msgs = swap(call(add_up, sds(NH, 216, BLOCK), msgs, first, second), "y")
    outs = [sds(16, 16, 512), sds(BLOCK, D), sds(NZ, D)]
    msgs, first, second = call(state_parts, outs, msgs, q, sq, w_out, keys, values)
    msgs = swap(msgs, ("zl",) + PLANE)
    back = swap(call(regroup, sds(NZ, 88, BLOCK), msgs, first, second), Z)
    states = swap(call(reduce_states, sds(2 * NP, 16, 512), back), ("zl",) + PLANE)
    outs = [sds(BLOCK, D)] + [sds(BLOCK, HD)] * 3
    return tuple(call(finish, outs, states, back, e, w_out, keys, values, home=4))


def solution(mesh):
    finer = Mesh(mesh.devices.reshape(8, 2, 4, 2, mesh.shape["head"]), ("zh", "zl", "x", "c", "y"))
    return jax.shard_map(
        shards,
        mesh=finer,
        in_specs=(
            P(SEQ, "y"),
            P(SEQ),
            P(None, SEQ),
            P(SEQ, None, "y"),
            P(SEQ, "y", None),
            P(SEQ, "y"),
            P(SEQ, "y"),
            P(SEQ, "y"),
            P(SEQ, "y"),
            P("y", None),
        ),
        out_specs=(P(SEQ, None), P(SEQ, "y"), P(SEQ, "y"), P(SEQ, "y")),
        check_vma=False,
    )
```
